32 devices in a mesh: lon: 4 (over y, core), lat: 8 (over z, x).
Axes of the slice: x: 2, y: 2, z: 4, core: 2. Of those that a mesh axis runs over, the one named last changes fastest.
Arguments:
- thermal_deviation: float32 [32, 32, 512], P(None, 'lat', 'lon'), may hold values from -5 to 5
- moisture_deviation: float32 [32, 32, 512], P(None, 'lat', 'lon'), may hold values from -5 to 5
- eastward_stability: float32 [32, 32, 512], P(None, 'lat', 'lon'), may hold values from -0.5 to 0.5
- northward_stability: float32 [32, 32, 512], P(None, 'lat', 'lon'), may hold values from -0.4 to 0.4
- sun_height_ratio: float32 [32, 512], P('lat', 'lon'), may hold values from 0.25 to 1
- extinction_coeff: float32 [112, 32], replicated, may hold values from 0.005 to 0.05
- reflectivity_ratio: float32 [112], replicated, may hold values from 0.1 to 0.9
- insolation_source: float32 [112], replicated, may hold values from 0.05 to 0.5
- daylight_tally: int32 [8, 4], P('lat', 'lon'), may hold values from 0 to 512, as said below
- daylight_permutation: int32 [8, 4, 512], P('lat', 'lon'), may hold values from 0 to 511, as said below
Outputs:
- temperature_next: float32 [32, 32, 512], P(None, 'lat', 'lon')
- humidity_next: float32 [32, 32, 512], P(None, 'lat', 'lon')
- warming_tendency: float32 [32, 32, 512], P(None, 'lat', 'lon')
The draws below stay inside these ranges and needn't reach their ends.
Inputs may be any that keep to these rules, and one draw needn't show every extreme that they name: `daylight_tally`: the block at longitude block j and the one at j + 2 in the same latitude band together have exactly 512 sunlit columns; some block has all 512 sunlit and some has none. `daylight_permutation`: each block's list is an ordering of its 512 local column indices; its first entries, as many as the block's sunlit count, are its sunlit columns.
All inputs are finite; a program needn't handle non-finite values.
Results may differ from the reference program's by a relative error of at most 0.0003.
Values sent between devices are 32-bit elements; how exact they have to be, the bound alone decides.
No kernel may reach another device: no remote copies, remote signals or barrier semaphores. Data moves between devices by JAX's collectives and lax.ppermute only.
A program may use at most 64 MiB of HBM per device.

```python
import math
import jax
import jax.numpy as jnp
from jax import lax

CLAT = 4
CLON = 128
STRATA_TOTAL = 32
G = 112
COLS = 512
MERIDIAN_SPAN = 32
PARALLEL_SPAN = 512
BLK_LAT = 8
BLK_LON = 4


def sunlit_plan(key):
    base_key = jax.random.fold_in(key, 7301)
    count_key, order_key = jax.random.split(base_key)
    first_half = jax.random.randint(count_key, (BLK_LAT, BLK_LON // 2), 0, COLS + 1, dtype=jnp.int32)
    first_half = first_half.at[0, 0].set(COLS).at[BLK_LAT - 1, BLK_LON // 2 - 1].set(0)
    counts = jnp.concatenate([first_half, COLS - first_half], axis=1)
    key_list = jax.random.split(order_key, BLK_LAT * BLK_LON)
    orders = jax.vmap(lambda single: jax.random.permutation(single, jnp.arange(COLS, dtype=jnp.int32)))(key_list)
    return (counts.astype(jnp.int32), orders.reshape(BLK_LAT, BLK_LON, COLS).astype(jnp.int32))


def draw_daylight_tally(key, part):
    return sunlit_plan(key)[0]


def draw_daylight_permutation(key, part):
    return sunlit_plan(key)[1]


def block_scale(rng, dims, shards, low, largest):
    gain = 1.0
    for axis_at, parts in shards:
        heights = jax.random.uniform(jax.random.fold_in(jax.random.fold_in(rng, 6), axis_at), (parts,), jnp.float32, low / len(shards), largest / len(shards))
        gain = gain * jnp.repeat(jnp.exp(heights), dims[axis_at] // parts).reshape((-1,) + (1,) * (len(dims) - 1 - axis_at))
    return gain


def scatter_about(stream_key, dims, width, limit, cuts=(), kind=jnp.bfloat16):
    drawn = width * jax.random.normal(stream_key, dims, jnp.float32)
    if cuts:
        drawn = drawn * block_scale(stream_key, dims, cuts, -0.22, 0.18)
    return jnp.clip(drawn, -limit, limit).astype(kind)


def setup_inputs(seed: int = 0) -> dict:
    keys = jax.random.split(jax.random.key(seed), 11)
    return {
        "thermal_deviation": scatter_about(keys[0], (STRATA_TOTAL, MERIDIAN_SPAN, PARALLEL_SPAN), 1.0, 5.0, ((1, 8), (2, 4)), jnp.float32),
        "moisture_deviation": scatter_about(keys[1], (STRATA_TOTAL, MERIDIAN_SPAN, PARALLEL_SPAN), 1.0, 5.0, ((1, 8), (2, 4)), jnp.float32),
        "eastward_stability": jnp.clip(jax.random.uniform(keys[2], (STRATA_TOTAL, MERIDIAN_SPAN, PARALLEL_SPAN), jnp.float32, -0.5, 0.5) * block_scale(keys[2], (STRATA_TOTAL, MERIDIAN_SPAN, PARALLEL_SPAN), ((1, 8), (2, 4)), -0.4, 0.0), -0.5, 0.5),
        "northward_stability": jnp.clip(jax.random.uniform(keys[3], (STRATA_TOTAL, MERIDIAN_SPAN, PARALLEL_SPAN), jnp.float32, -0.4, 0.4) * block_scale(keys[3], (STRATA_TOTAL, MERIDIAN_SPAN, PARALLEL_SPAN), ((1, 8), (2, 4)), -0.4, 0.0), -0.4, 0.4),
        "sun_height_ratio": jnp.clip(0.25 + 0.75 * jax.random.uniform(keys[4], (MERIDIAN_SPAN, PARALLEL_SPAN), jnp.float32) ** block_scale(keys[4], (MERIDIAN_SPAN, PARALLEL_SPAN), ((0, 8), (1, 4)), -0.2, 0.2), 0.25, 1.0),
        "extinction_coeff": jnp.clip(jnp.exp(jax.random.uniform(keys[5], (G, STRATA_TOTAL), jnp.float32, math.log(0.005), math.log(0.05))), 0.005, 0.05),
        "reflectivity_ratio": jnp.clip(jax.random.uniform(keys[6], (G,), jnp.float32, 0.1, 0.9), 0.1, 0.9),
        "insolation_source": jnp.clip(jnp.exp(jax.random.uniform(keys[7], (G,), jnp.float32, math.log(0.05), math.log(0.5))), 0.05, 0.5),
        "daylight_tally": draw_daylight_tally(jax.random.fold_in(keys[10], 71), 0),
        "daylight_permutation": draw_daylight_permutation(jax.random.fold_in(keys[10], 71), 0),
    }


heat_coeff = 20.0


def advect(quantity_group, courant_x, courant_y):
    eastern = jnp.roll(quantity_group, -1, axis=3)
    western = jnp.roll(quantity_group, 1, axis=3)
    northern = jnp.concatenate([quantity_group[:, :, 1:], quantity_group[:, :, -1:]], axis=2)
    southern = jnp.concatenate([quantity_group[:, :, :1], quantity_group[:, :, :-1]], axis=2)
    return (quantity_group - 0.5 * courant_x * (eastern - western)
            + 0.5 * courant_x * courant_x * (eastern - 2.0 * quantity_group + western)
            - 0.5 * courant_y * (northern - southern)
            + 0.5 * courant_y * courant_y * (northern - 2.0 * quantity_group + southern))


def thomas_solve(lower_band, diagonal, upper_band, source):
    zero_row = jnp.zeros_like(source[0])

    def forward(carry, level_data):
        prev_c, prev_d = carry
        level_lower, level_diag, level_upper, level_rhs = level_data
        denom_val = level_diag + level_lower * prev_c
        new_c = -level_upper / denom_val
        new_d = (level_rhs + level_lower * prev_d) / denom_val
        return (new_c, new_d), (new_c, new_d)

    _, primes = lax.scan(forward, (zero_row, zero_row), (lower_band, diagonal, upper_band, source))

    def backward(following, level_data):
        prime_c, prime_d = level_data
        value_now = prime_d - prime_c * following
        return value_now, value_now

    _, solution = lax.scan(backward, zero_row, primes, reverse=True)
    return solution


def column_heating(temp_cols, hum_cols, cos_cols, extinction_coeff, reflectivity_ratio, insolation_source, solver):
    stratum_group = temp_cols.shape[0]
    factor = (1.5 + jnp.tanh(hum_cols)) * (1.0 + 0.25 * jnp.tanh(temp_cols))
    gblock = 16
    count_blocks = extinction_coeff.shape[0] // gblock
    blocks = (extinction_coeff.reshape(count_blocks, gblock, stratum_group),
              reflectivity_ratio.reshape(count_blocks, gblock),
              insolation_source.reshape(count_blocks, gblock))

    def one_block(block):
        block_absorb, block_albedo, block_solar = block
        optical = jnp.transpose(block_absorb)[:, :, None] * factor[:, None, :]
        path_depth = jnp.cumsum(optical, axis=0) - 0.5 * optical
        direct = block_solar[None, :, None] * cos_cols[None, None, :] * jnp.exp(-path_depth / cos_cols[None, None, :])
        source = block_albedo[None, :, None] * direct
        coupling = 2.0 / (1.0 + 3.0 * (optical[:-1] + optical[1:]))
        edge_row = jnp.zeros_like(optical[:1])
        upper_band = jnp.concatenate([coupling, edge_row], axis=0)
        lower_band = jnp.concatenate([edge_row, coupling], axis=0)
        absorbed = (1.0 - block_albedo)[None, :, None] * optical
        diagonal = 0.5 + upper_band + lower_band + absorbed
        diffuse = solver(lower_band, diagonal, upper_band, source)
        return jnp.sum(absorbed * (diffuse + direct), axis=1)

    return heat_coeff * jnp.sum(lax.map(one_block, blocks), axis=0)


def reference(thermal_deviation, moisture_deviation, eastward_stability, northward_stability, sun_height_ratio, extinction_coeff, reflectivity_ratio, insolation_source, daylight_tally, daylight_permutation):
    quantity_group = jnp.stack([thermal_deviation, moisture_deviation])
    for repeat in range(2):
        quantity_group = advect(quantity_group, eastward_stability, northward_stability)
    blocks_lat, blocks_lon, profile_group = daylight_permutation.shape
    slots = jnp.arange(profile_group, dtype=jnp.int32)
    partition_identifiers = jax.vmap(jax.vmap(lambda listing: jnp.zeros((profile_group,), jnp.int32).at[listing].set(slots)))(daylight_permutation)
    lit_mask = partition_identifiers < daylight_tally[:, :, None]
    lit_mask = lit_mask.reshape(blocks_lat, blocks_lon, CLAT, CLON).transpose(0, 2, 1, 3).reshape(MERIDIAN_SPAN, PARALLEL_SPAN)
    parallel_entries = (jnp.transpose(thermal_deviation, (1, 0, 2)), jnp.transpose(moisture_deviation, (1, 0, 2)), sun_height_ratio)
    heat_rows = lax.map(lambda row_item: column_heating(row_item[0], row_item[1], row_item[2], extinction_coeff, reflectivity_ratio, insolation_source, thomas_solve), parallel_entries)
    warming_tendency = jnp.where(lit_mask[None], jnp.transpose(heat_rows, (1, 0, 2)), 0.0)
    return quantity_group[0], quantity_group[1], warming_tendency
```

```python
import math

import jax
import jax.numpy as jnp
import numpy as np
from jax import lax
from jax.experimental import pallas as pl
from jax.experimental.pallas import tpu as pltpu
from jax.sharding import PartitionSpec as P

heat_coeff = 20.0
f32, bf16 = jnp.float32, jnp.bfloat16
VMEM_SPEC = pl.BlockSpec(memory_space=pltpu.VMEM)
SMEM_SPEC = pl.BlockSpec(memory_space=pltpu.SMEM)
NT_DIMS = (((1,), (1,)), ((), ()))
TN_DIMS = (((0,), (0,)), ((), ()))


def iota(shape, dim):
    return lax.broadcasted_iota(jnp.int32, shape, dim)


def shape_of(*dims):
    return jax.ShapeDtypeStruct(dims, f32)


def swaps(count, first, ring):
    pairs = []
    for i in range(first, count, 2):
        j = i + 1
        if j == count and not ring:
            break
        pairs += [(i, j % count), (j % count, i)]
    return pairs


def rows_kernel(t, q, cx, cy, tally, perm, to_a, to_b, lit):
    total, lanes = t.shape
    rows = lit.shape[0]
    levels = total // rows
    even = lax.rem(lax.axis_index("lat"), 2) == 0

    def row(ref, r):
        return ref[pl.ds(r, levels, stride=rows), :]

    top = rows - 1
    picks = ((t, 0), (t, 1), (q, 0), (q, 1), (cx, 0), (cy, 0))
    for k, (ref, deep) in enumerate(picks):
        high, low = row(ref, top - deep), row(ref, deep)
        to_a[k * levels : (k + 1) * levels, :] = jnp.where(even, high, low)
        to_b[k * levels : (k + 1) * levels, :] = jnp.where(even, low, high)
    count = tally[0, 0]
    found = jnp.zeros((8, lanes), f32)
    for r in range(rows):
        column = perm[0, :, r * lanes : (r + 1) * lanes]
        row_at = column // lanes
        lane_at = column - row_at * lanes
        sunlit = iota((1, lanes), 1) + r * lanes < count
        at_row = jnp.where((row_at == iota((8, lanes), 0)) & sunlit, 1.0, 0.0).astype(bf16)
        at_lane = jnp.where(lane_at == iota((lanes, lanes), 0), 1.0, 0.0).astype(bf16)
        found += lax.dot_general(at_row, at_lane, NT_DIMS, preferred_element_type=f32)
    lit[...] = found[:rows]


def edge_rows(t, q, cx, cy, tally, perm, rows):
    total, lanes = t.shape
    levels = total // rows
    return pl.pallas_call(
        rows_kernel,
        out_shape=(shape_of(6 * levels, lanes), shape_of(6 * levels, lanes), shape_of(rows, lanes)),
        in_specs=[VMEM_SPEC] * 4 + [SMEM_SPEC, VMEM_SPEC],
        out_specs=(VMEM_SPEC,) * 3,
        name="edge_rows",
    )(t, q, cx, cy, tally, perm)


def columns_kernel(pad, t, q, cx, cy, from_a, from_b, ft, fq, fx, fy, own, to_a, to_b):
    total, lanes = t.shape
    levels = from_a.shape[0] // 6
    rows = total // levels
    tall = rows + 2 * pad
    lat = lax.axis_index("lat")
    even = lax.rem(lat, 2) == 0
    first, last = lat == 0, lat == lax.axis_size("lat") - 1
    outs = (ft, fq, fx, fy)
    refs = (t, q, cx, cy)
    slots = ((0, 1), (2, 3), (4,), (5,))
    for ref, out, at in zip(refs, outs, slots):
        inner = [ref[pl.ds(r, levels, stride=rows), :] for r in range(rows)]
        for r in range(rows):
            out[pl.ds(pad + r, levels, stride=tall), :] = inner[r]
        for deep in range(pad):
            k = at[min(deep, len(at) - 1)]
            a = from_a[k * levels : (k + 1) * levels, :]
            b = from_b[k * levels : (k + 1) * levels, :]
            south = jnp.where(first, inner[0], jnp.where(even, b, a))
            north = jnp.where(last, inner[rows - 1], jnp.where(even, a, b))
            out[pl.ds(pad - 1 - deep, levels, stride=tall), :] = south
            out[pl.ds(pad + rows + deep, levels, stride=tall), :] = north
    edges = jnp.zeros((16, levels * tall), f32)
    which = iota((16, lanes), 0)
    lane = iota((16, lanes), 1)
    for out, at in zip(outs, slots):
        pick = jnp.zeros((16, lanes), jnp.bool_)
        for deep, k in enumerate(at):
            pick |= (which == k) & (lane == lanes - 1 - deep)
            pick |= (which == 8 + k) & (lane == deep)
        edges += lax.dot_general(
            jnp.where(pick, 1.0, 0.0),
            out[...],
            NT_DIMS,
            precision=lax.Precision.HIGHEST,
            preferred_element_type=f32,
        )
    own[...] = edges
    even_lon = lax.rem(lax.axis_index("lon"), 2) == 0
    east, west = edges[:8], edges[8:]
    to_a[...] = jnp.where(even_lon, east, west)
    to_b[...] = jnp.where(even_lon, west, east)


def edge_columns(t, q, cx, cy, from_a, from_b, pad):
    import functools

    total, lanes = t.shape
    levels = from_a.shape[0] // 6
    tall = levels * (total // levels + 2 * pad)
    return pl.pallas_call(
        functools.partial(columns_kernel, pad),
        out_shape=(*[shape_of(tall, lanes)] * 4, shape_of(16, tall), shape_of(8, tall), shape_of(8, tall)),
        in_specs=[VMEM_SPEC] * 6,
        out_specs=(VMEM_SPEC,) * 7,
        name="edge_columns",
    )(t, q, cx, cy, from_a, from_b)


def weights(cx, cy):
    hx, hy = 0.5 * cx, 0.5 * cy
    sx, sy = hx * cx, hy * cy
    return 1.0 - 2.0 * (sx + sy), sx - hx, sx + hx, sy - hy, sy + hy


def blend(w, here, east, west, north, south):
    return w[0] * here + w[1] * east + w[2] * west + w[3] * north + w[4] * south


def advect_kernel(rows, pad, ft, fq, fx, fy, own, from_a, from_b, t_out, q_out, keep):
    tall, lanes = ft.shape
    high = rows + 2 * pad
    levels = tall // high
    even_lon = lax.rem(lax.axis_index("lon"), 2) == 0
    lat = lax.axis_index("lat")
    first, last = lat == 0, lat == lax.axis_size("lat") - 1
    a, b = from_a[...], from_b[...]
    east, west = jnp.where(even_lon, a, b), jnp.where(even_lon, b, a)
    mine = own[...]

    def strip(x, k):
        return x[k : k + 1, :]

    halo = []
    firsts = []
    ww = weights(strip(west, 4), strip(west, 5))
    we = weights(strip(east, 4), strip(east, 5))
    for k in (0, 2):
        near_w, near_e = strip(west, k), strip(east, k)
        halo += [near_w, near_e]
        up = lambda x: pltpu.roll(x, tall - 1, 1)
        down = lambda x: pltpu.roll(x, 1, 1)
        firsts.append(blend(ww, near_w, strip(mine, 8 + k), strip(west, k + 1), up(near_w), down(near_w)))
        firsts.append(blend(we, near_e, strip(east, k + 1), strip(mine, k), up(near_e), down(near_e)))
    stack = jnp.concatenate(halo + firsts, axis=0)
    source, target = iota((8, 4 * lanes), 0), iota((8, 4 * lanes), 1)
    wanted = (source // 2) * lanes + lax.rem(source, 2) * (lanes - 1)
    rims = lax.dot_general(
        stack,
        jnp.where(target == wanted, 1.0, 0.0),
        TN_DIMS,
        precision=lax.Precision.HIGHEST,
        preferred_element_type=f32,
    )
    cut = lambda x: x.reshape(levels, high, lanes)
    w = weights(cut(fx[...]), cut(fy[...]))
    full = (levels, high, lanes)
    lane, at = iota(full, 2), iota(full, 1)
    for k, (ref, out) in enumerate(((ft, t_out), (fq, q_out))):
        f = cut(ref[...])
        for step in range(2):
            rim = cut(rims[:, (2 * step + k) * lanes : (2 * step + k + 1) * lanes])
            e = jnp.where(lane == lanes - 1, rim, pltpu.roll(f, lanes - 1, 2))
            wst = jnp.where(lane == 0, rim, pltpu.roll(f, 1, 2))
            n = jnp.where(last & (at == pad + rows - 1), f, pltpu.roll(f, high - 1, 1))
            s = jnp.where(first & (at == pad), f, pltpu.roll(f, 1, 1))
            f = blend(w, f, e, wst, n, s)
        keep[...] = f.reshape(tall, lanes)
        for r in range(rows):
            out[pl.ds(r, levels, stride=rows), :] = keep[pl.ds(pad + r, levels, stride=high), :]


def advect(ft, fq, fx, fy, own, from_a, from_b, rows, pad):
    import functools

    tall, lanes = ft.shape
    total = tall // (rows + 2 * pad) * rows
    return pl.pallas_call(
        functools.partial(advect_kernel, rows, pad),
        out_shape=(shape_of(total, lanes), shape_of(total, lanes)),
        in_specs=[VMEM_SPEC] * 7,
        out_specs=(VMEM_SPEC,) * 2,
        scratch_shapes=[pltpu.VMEM((tall, lanes), f32)],
        name="advect",
    )(ft, fq, fx, fy, own, from_a, from_b)


def halves(x):
    high = x.astype(bf16)
    return high, (x - high.astype(f32)).astype(bf16)


def thirds(value):
    import ml_dtypes

    left, parts = np.float32(value), []
    for _ in range(3):
        part = np.float32(left.astype(ml_dtypes.bfloat16))
        parts.append(float(part))
        left = np.float32(left - part)
    return parts


SLOTS, AHEAD = 16, 8


def heating_kernel(
    t, q, mu, k, albedo, solar, lit, out,
    factor, linear, tables, masks, shares, albedos, trans, pull, beam, total,
):
    levels, gpoints = k.shape[1], k.shape[0]
    rows, lanes = mu.shape
    quarter = lanes // 4
    wide = 2 * lanes
    engines = rows // 2
    factor[...] = (1.5 + jnp.tanh(q[...])) * (1.0 + 0.25 * jnp.tanh(t[...]))
    ones = jnp.ones((quarter, lanes), bf16)
    for r in range(rows):
        level_factor = factor[pl.ds(r, levels, stride=rows), :]
        per_path = level_factor * (-math.log2(math.e) / mu[r : r + 1, :])
        for start, value in ((0, level_factor), (lanes, per_path)):
            high, low = halves(value)
            linear[start : start + lanes, r * lanes : (r + 1) * lanes] = jnp.concatenate(
                [high, high, low, ones], axis=0
            )
    square = iota((gpoints, gpoints), 0) == iota((gpoints, gpoints), 1)

    def upright(row):
        return jnp.sum(jnp.where(square, row, 0.0), axis=1, keepdims=True)

    w = upright(albedo[...])
    coeff = k[...]
    slot = iota((1, quarter), 1)

    def table(value, constants):
        high = value.astype(bf16).astype(f32)
        tail = jnp.zeros((1, quarter), f32)
        for i, c in enumerate(constants):
            tail = jnp.where(slot == i, c, tail)
        tail = jnp.broadcast_to(tail, (gpoints, quarter))
        return jnp.concatenate([high, value - high, high, tail], axis=1).astype(bf16)

    tables[0] = table(coeff, thirds(1.0 / 3.0))
    tables[1] = table(1.5 * (1.0 - w) * coeff, (0.75,))
    shares[...] = (1.0 - w) * upright(solar[...]) * coeff
    albedos[...] = jnp.broadcast_to(1.5 * w, (gpoints, lanes))
    lane = iota((16, lanes), 1)
    level, constant = lax.rem(lane, quarter), lane >= 3 * quarter
    for l in range(levels):
        masks[0, l] = jnp.where(constant | (level == l) | (level == l + 1), 1.0, 0.0).astype(bf16)
        masks[1, l] = jnp.where(constant | (level == l), 1.0, 0.0).astype(bf16)
        masks[2, l] = jnp.where(
            constant, 0.0, jnp.where(level < l, 1.0, jnp.where(level == l, 0.5, 0.0))
        ).astype(bf16)
    total[...] = jnp.zeros_like(total)
    units = [(a, b) for a in range(2) for b in range(rows)]
    each = range(len(units))

    def main(*sums):
        def at(m, l):
            return sums[m * SLOTS + l % SLOTS]

        def group(i):
            start = pl.multiple_of(i * 16, 16)
            starts = [pl.multiple_of(start + 8 * a, 8) for a in range(2)]
            plain, absorbing = (tables[j, pl.ds(start, 16), :] for j in range(2))
            w15 = [albedos[pl.ds(s, 8), :] for s in starts]
            share = [shares[pl.ds(s, 8), :] for s in starts]
            blank = jnp.zeros((16, lanes), bf16)

            def issue(l):
                stack = [
                    jnp.concatenate([plain * masks[0, l], blank], axis=1),
                    jnp.concatenate([absorbing * masks[1, l], blank], axis=1),
                    jnp.concatenate([blank, plain * masks[2, l]], axis=1),
                ]
                stack = jnp.concatenate(stack, axis=0)
                for m in range(engines):
                    pltpu.matmul_acc_lhs(at(m, l), stack)

            for l in range(AHEAD):
                issue(l)
            y = current = step = None
            for l in range(levels):
                if l + AHEAD < levels:
                    issue(l + AHEAD)
                popped = [pltpu.matmul_pop(at(m, l)) for m in range(engines)]

                def part(kind, a, b):
                    s = kind * 16 + a * 8
                    return popped[b // 2][s : s + 8, (b % 2) * lanes : (b % 2 + 1) * lanes]

                resist, shunt, path = ([part(i, a, b) for a, b in units] for i in range(3))
                direct = [jnp.exp2(p) for p in path]
                source = [w15[units[u][0]] * direct[u] for u in each]
                for u in each:
                    beam[u, l] = direct[u]
                if l == 0:
                    y, current = shunt, source
                else:
                    y = [shunt[u] + y[u] * step[u] for u in each]
                    current = [source[u] + current[u] * step[u] for u in each]
                if l < levels - 1:
                    step = [1.0 / (1.0 + resist[u] * y[u]) for u in each]
                    for u in each:
                        trans[u, l] = step[u]
                        pull[u, l] = resist[u] * current[u]
            diffuse = [current[u] / y[u] for u in each]
            for l in range(levels - 1, -1, -1):
                if l < levels - 1:
                    diffuse = [trans[u, l] * (pull[u, l] + diffuse[u]) for u in each]
                spread = [jnp.broadcast_to(share[a][:, l : l + 1], (8, lanes)) for a in range(2)]
                for b in range(rows):
                    pair = [
                        (diffuse[a * rows + b] + beam[a * rows + b, l]) * spread[a]
                        for a in range(2)
                    ]
                    total[l, b] = total[l, b] + (pair[0] + pair[1])

        nothing = jnp.zeros((16, wide), bf16)
        for m in range(engines):
            last = sums[engines * SLOTS + m]
            pltpu.matmul_push_rhs(linear[:, m * wide : (m + 1) * wide], 0, m)
            pltpu.matmul_acc_lhs(last, nothing, load_staged_rhs=0)
            pltpu.matmul_pop(last)
        pl.loop(0, gpoints // 16)(group)

    pl.run_scoped(
        main,
        *[pltpu.ACC(m)((48, wide), f32) for m in range(engines) for _ in range(SLOTS)],
        *[pltpu.ACC(m)((16, wide), f32) for m in range(engines)],
    )
    scale = heat_coeff * mu[...] * lit[...]
    for l in range(levels):
        here = pl.ds(l * rows, rows)
        out[here, :] = jnp.sum(total[l], axis=1) * scale * factor[here, :]


def heating(t, q, mu, k, albedo, solar, lit):
    rows, lanes = mu.shape
    gpoints, levels = k.shape
    units = 2 * rows
    stage = pltpu.VMEM((units, levels, 8, lanes), f32)
    return pl.pallas_call(
        heating_kernel,
        out_shape=shape_of(*t.shape),
        in_specs=[VMEM_SPEC] * 7,
        out_specs=VMEM_SPEC,
        scratch_shapes=[
            pltpu.VMEM(t.shape, f32),
            pltpu.VMEM((2 * lanes, rows * lanes), bf16),
            pltpu.VMEM((2, gpoints, lanes), bf16),
            pltpu.VMEM((3, levels, 16, lanes), bf16),
            pltpu.VMEM((gpoints, levels), f32),
            pltpu.VMEM((gpoints, lanes), f32),
            stage,
            stage,
            stage,
            pltpu.VMEM((levels, rows, 8, lanes), f32),
        ],
        cost_estimate=pl.CostEstimate(
            flops=40 * gpoints * levels * rows * lanes * 16, bytes_accessed=1 << 20, transcendentals=2 * gpoints * levels * rows * lanes
        ),
        name="heating",
    )(t, q, mu, k, albedo, solar, lit)


def local(
    thermal_deviation,
    moisture_deviation,
    eastward_stability,
    northward_stability,
    sun_height_ratio,
    extinction_coeff,
    reflectivity_ratio,
    insolation_source,
    daylight_tally,
    daylight_permutation,
):
    levels, rows, lanes = thermal_deviation.shape
    pad = 2
    lat_count, lon_count = lax.axis_size("lat"), lax.axis_size("lon")
    flat = lambda x: x.reshape(levels * rows, lanes)
    t, q, cx, cy = (
        flat(x)
        for x in (thermal_deviation, moisture_deviation, eastward_stability, northward_stability)
    )
    to_a, to_b, lit = edge_rows(t, q, cx, cy, daylight_tally, daylight_permutation, rows)
    lat_b = lax.ppermute(to_b, "lat", swaps(lat_count, 1, False))
    lat_a = lax.ppermute(to_a, "lat", swaps(lat_count, 0, False))
    warming = heating(
        t,
        q,
        sun_height_ratio,
        extinction_coeff,
        reflectivity_ratio.reshape(1, -1),
        insolation_source.reshape(1, -1),
        lit,
    )
    ft, fq, fx, fy, own, to_a, to_b = edge_columns(t, q, cx, cy, lat_a, lat_b, pad)
    lon_b = lax.ppermute(to_b, "lon", swaps(lon_count, 1, True))
    lon_a = lax.ppermute(to_a, "lon", swaps(lon_count, 0, True))
    t_next, q_next = advect(ft, fq, fx, fy, own, lon_a, lon_b, rows, pad)
    whole = lambda x: x.reshape(levels, rows, lanes)
    return whole(t_next), whole(q_next), whole(warming)


def solution(mesh):
    volume, surface = P(None, "lat", "lon"), P("lat", "lon")
    placed = (volume,) * 4 + (surface, P(), P(), P(), surface, P("lat", "lon", None))
    step = jax.shard_map(
        local, mesh=mesh, in_specs=placed, out_specs=(volume,) * 3, check_vma=False
    )
    return step
```

```python
import functools
import math

import jax
import jax.numpy as jnp
import ml_dtypes
import numpy as np
from jax import lax
from jax.experimental import pallas as pl
from jax.experimental.pallas import tpu as pltpu
from jax.sharding import PartitionSpec as P

heat_coeff = 20.0
f32, bf16 = jnp.float32, jnp.bfloat16
HELD = pltpu.VMEM
VMEM_SPEC = pl.BlockSpec(memory_space=pltpu.VMEM)
SMEM_SPEC = pl.BlockSpec(memory_space=pltpu.SMEM)
NT_DIMS = (((1,), (1,)), ((), ()))
TN_DIMS = (((0,), (0,)), ((), ()))


def iota(shape, dim):
    return lax.broadcasted_iota(jnp.int32, shape, dim)


def shape_of(*dims):
    return jax.ShapeDtypeStruct(dims, f32)


def held(*arrays):
    return [pltpu.with_memory_space_constraint(x, pltpu.VMEM) for x in arrays]


def swaps(count, first, ring):
    pairs = []
    for i in range(first, count, 2):
        j = i + 1
        if j == count and not ring:
            break
        pairs += [(i, j % count), (j % count, i)]
    return pairs


def rows_kernel(rows, t, q, cx, cy, to_a, to_b):
    levels = t.shape[0] // rows
    even = lax.rem(lax.axis_index("lat"), 2) == 0

    def row(ref, r):
        return ref[pl.ds(r, levels, stride=rows), :]

    picks = ((t, 0), (t, 1), (q, 0), (q, 1), (cx, 0), (cy, 0))
    for k, (ref, deep) in enumerate(picks):
        high, low = row(ref, rows - 1 - deep), row(ref, deep)
        to_a[k * levels : (k + 1) * levels, :] = jnp.where(even, high, low)
        to_b[k * levels : (k + 1) * levels, :] = jnp.where(even, low, high)


def edge_rows(t, q, cx, cy, rows):
    total, lanes = t.shape
    shape = (6 * (total // rows), lanes)
    return pl.pallas_call(
        functools.partial(rows_kernel, rows),
        out_shape=(HELD(shape, f32),) * 2,
        in_specs=[VMEM_SPEC] * 4,
        out_specs=(VMEM_SPEC,) * 2,
        name="edge_rows",
    )(t, q, cx, cy)


def halves(x):
    high = x.astype(bf16)
    return high, (x - high.astype(f32)).astype(bf16)


def thirds(value):
    left, parts = np.float32(value), []
    for _ in range(3):
        part = np.float32(left.astype(ml_dtypes.bfloat16))
        parts.append(float(part))
        left = np.float32(left - part)
    return parts


def pick_edges(slots, lanes, blocks):
    which, lane = iota((16, lanes), 0), iota((16, lanes), 1)
    edges = None
    for block, at in zip(blocks, slots):
        pick = jnp.zeros((16, lanes), jnp.bool_)
        for deep, k in enumerate(at):
            pick |= (which == k) & (lane == lanes - 1 - deep)
            pick |= (which == 8 + k) & (lane == deep)
        part = lax.dot_general(
            jnp.where(pick, 1.0, 0.0),
            block,
            NT_DIMS,
            precision=lax.Precision.HIGHEST,
            preferred_element_type=f32,
        )
        edges = part if edges is None else edges + part
    return edges


def prepare_kernel(
    pad, t, q, cx, cy, mu, k, albedo, solar, tally, perm,
    factor, linear, tables, masks, shares, albedos, scale, ft, fq, fx, fy, own,
):
    levels, gpoints = k.shape
    rows, lanes = mu.shape
    tall = rows + 2 * pad
    blocks = (t, q, cx, cy)
    for ref, out in zip(blocks, (ft, fq, fx, fy)):
        for r in range(rows):
            out[pl.ds(pad + r, levels, stride=tall), :] = ref[pl.ds(r, levels, stride=rows), :]
    own[...] = pick_edges(((0, 1), (2, 3), (4,), (5,)), lanes, [ref[...] for ref in blocks])

    count = tally[0, 0]
    found = jnp.zeros((8, lanes), f32)
    for r in range(rows):
        column = perm[0, :, r * lanes : (r + 1) * lanes]
        row_at = column // lanes
        lane_at = column - row_at * lanes
        sunlit = iota((1, lanes), 1) + r * lanes < count
        at_row = jnp.where((row_at == iota((8, lanes), 0)) & sunlit, 1.0, 0.0).astype(bf16)
        at_lane = jnp.where(lane_at == iota((lanes, lanes), 0), 1.0, 0.0).astype(bf16)
        found += lax.dot_general(at_row, at_lane, NT_DIMS, preferred_element_type=f32)
    scale[...] = heat_coeff * mu[...] * found[:rows]

    quarter = lanes // 4
    factor[...] = (1.5 + jnp.tanh(q[...])) * (1.0 + 0.25 * jnp.tanh(t[...]))
    ones = jnp.ones((quarter, lanes), bf16)
    for r in range(rows):
        level_factor = factor[pl.ds(r, levels, stride=rows), :]
        per_path = level_factor * (-math.log2(math.e) / mu[r : r + 1, :])
        for start, value in ((0, level_factor), (lanes, per_path)):
            high, low = halves(value)
            linear[start : start + lanes, r * lanes : (r + 1) * lanes] = jnp.concatenate(
                [high, high, low, ones], axis=0
            )
    square = iota((gpoints, gpoints), 0) == iota((gpoints, gpoints), 1)

    def upright(row):
        return jnp.sum(jnp.where(square, row, 0.0), axis=1, keepdims=True)

    w = upright(albedo[...])
    filled = jnp.concatenate([k[...], jnp.zeros((levels, lanes - gpoints), f32)], axis=1)
    coeff = jnp.transpose(filled)[:gpoints]
    slot = iota((1, quarter), 1)

    def table(value, constants):
        high = value.astype(bf16).astype(f32)
        tail = jnp.zeros((1, quarter), f32)
        for i, c in enumerate(constants):
            tail = jnp.where(slot == i, c, tail)
        tail = jnp.broadcast_to(tail, (gpoints, quarter))
        return jnp.concatenate([high, value - high, high, tail], axis=1).astype(bf16)

    tables[0] = table(coeff, thirds(1.0 / 3.0))
    tables[1] = table(1.5 * (1.0 - w) * coeff, (0.75,))
    shares[...] = (1.0 - w) * upright(solar[...]) * coeff
    albedos[...] = jnp.broadcast_to(1.5 * w, (gpoints, lanes))
    lane = iota((16, lanes), 1)
    level, constant = lax.rem(lane, quarter), lane >= 3 * quarter
    for l in range(levels):
        masks[0, l] = jnp.where(constant | (level == l) | (level == l + 1), 1.0, 0.0).astype(bf16)
        masks[1, l] = jnp.where(constant | (level == l), 1.0, 0.0).astype(bf16)
        masks[2, l] = jnp.where(
            constant, 0.0, jnp.where(level < l, 1.0, jnp.where(level == l, 0.5, 0.0))
        ).astype(bf16)


def prepare(t, q, cx, cy, mu, k, albedo, solar, tally, perm, pad):
    levels, gpoints = k.shape
    rows, lanes = mu.shape
    tall = levels * (rows + 2 * pad)
    return pl.pallas_call(
        functools.partial(prepare_kernel, pad),
        out_shape=(
            HELD(t.shape, f32),
            HELD((2 * lanes, rows * lanes), bf16),
            HELD((2, gpoints, lanes), bf16),
            HELD((3, levels, 16, lanes), bf16),
            HELD((gpoints, levels), f32),
            HELD((gpoints, lanes), f32),
            HELD((rows, lanes), f32),
            *[HELD((tall, lanes), f32)] * 4,
            HELD((16, levels * rows), f32),
        ),
        in_specs=[VMEM_SPEC] * 8 + [SMEM_SPEC, VMEM_SPEC],
        out_specs=(VMEM_SPEC,) * 12,
        cost_estimate=pl.CostEstimate(flops=1 << 22, bytes_accessed=1 << 21, transcendentals=1 << 17),
        name="prepare",
    )(t, q, cx, cy, mu, k, albedo, solar, tally, perm)


def by_side(even, first, last, from_a, from_b, k, levels, low, high):
    a, b = from_a[k * levels : (k + 1) * levels, :], from_b[k * levels : (k + 1) * levels, :]
    south, north = jnp.where(even, b, a), jnp.where(even, a, b)
    return jnp.where(first, low, south), jnp.where(last, high, north)


def lat_place():
    lat = lax.axis_index("lat")
    return lax.rem(lat, 2) == 0, lat == 0, lat == lax.axis_size("lat") - 1


def columns_kernel(pad, ft, fq, own, from_a, from_b, edges, to_a, to_b, ring):
    levels = from_a.shape[0] // 6
    total, lanes = ring.shape[1:]
    rows = total // levels
    tall = rows + 2 * pad
    ring[...] = jnp.zeros_like(ring)
    for i, ref in enumerate((ft, fq)):
        low, high = (ref[pl.ds(pad + r, levels, stride=tall), :] for r in (0, rows - 1))
        south, north = by_side(*lat_place(), from_a, from_b, 2 * i, levels, low, high)
        ring[i, pl.ds(0, levels, stride=rows), :] = south
        ring[i, pl.ds(rows - 1, levels, stride=rows), :] = north
    both = own[...] + pick_edges(((6,), (7,)), lanes, [ring[0], ring[1]])
    edges[...] = both
    even_lon = lax.rem(lax.axis_index("lon"), 2) == 0
    east, west = both[:8], both[8:]
    to_a[...] = jnp.where(even_lon, east, west)
    to_b[...] = jnp.where(even_lon, west, east)


def edge_columns(ft, fq, own, from_a, from_b, rows, pad):
    lanes = ft.shape[1]
    total = own.shape[1]
    return pl.pallas_call(
        functools.partial(columns_kernel, pad),
        out_shape=(HELD((16, total), f32), HELD((8, total), f32), HELD((8, total), f32)),
        in_specs=[VMEM_SPEC] * 5,
        out_specs=(VMEM_SPEC,) * 3,
        scratch_shapes=[pltpu.VMEM((2, total, lanes), f32)],
        name="edge_columns",
    )(*held(ft, fq, own, from_a, from_b))


def weights(cx, cy):
    hx, hy = 0.5 * cx, 0.5 * cy
    sx, sy = hx * cx, hy * cy
    return 1.0 - 2.0 * (sx + sy), sx - hx, sx + hx, sy - hy, sy + hy


def blend(w, here, east, west, north, south):
    return w[0] * here + w[1] * east + w[2] * west + w[3] * north + w[4] * south


def advect_kernel(
    rows, pad, ft, fq, fx, fy, edges, lat_a, lat_b, lon_a, lon_b, t_out, q_out, gt, gq, gx, gy, st, sq
):
    lanes = ft.shape[1]
    high = rows + 2 * pad
    levels = ft.shape[0] // high
    total = levels * rows
    place = lat_place()
    _, first, last = place
    grids = (gt, gq, gx, gy)
    for ref, grid, at in zip((ft, fq, fx, fy), grids, ((0, 1), (2, 3), (4,), (5,))):
        grid[...] = ref[...]
        low, top = (ref[pl.ds(pad + r, levels, stride=high), :] for r in (0, rows - 1))
        for deep in range(pad):
            k = at[min(deep, len(at) - 1)]
            south, north = by_side(*place, lat_a, lat_b, k, levels, low, top)
            grid[pl.ds(pad - 1 - deep, levels, stride=high), :] = south
            grid[pl.ds(pad + rows + deep, levels, stride=high), :] = north
    even_lon = lax.rem(lax.axis_index("lon"), 2) == 0
    a, b = lon_a[...], lon_b[...]
    east, west = jnp.where(even_lon, a, b), jnp.where(even_lon, b, a)
    mine = edges[...]

    def strip(x, k):
        return x[k : k + 1, :]

    row_of = lax.rem(iota((1, total), 1), rows)

    def up(x, k):
        return jnp.where(row_of == rows - 1, strip(x, 6 + k // 2), pltpu.roll(strip(x, k), total - 1, 1))

    def down(x, k):
        return jnp.where(row_of == 0, strip(x, 6 + k // 2), pltpu.roll(strip(x, k), 1, 1))

    ww = weights(strip(west, 4), strip(west, 5))
    we = weights(strip(east, 4), strip(east, 5))
    firsts = []
    for k in (0, 2):
        firsts.append(blend(ww, strip(west, k), strip(mine, 8 + k), strip(west, k + 1), up(west, k), down(west, k)))
        firsts.append(blend(we, strip(east, k), strip(east, k + 1), strip(mine, k), up(east, k), down(east, k)))
    stack = jnp.concatenate(
        [strip(x, k) for k in (0, 2, 6, 7) for x in (west, east)] + firsts + [jnp.zeros((4, total), f32)],
        axis=0,
    )
    source, target = iota((16, 6 * lanes), 0), iota((16, 6 * lanes), 1)
    wanted = (source // 2) * lanes + lax.rem(source, 2) * (lanes - 1)
    rims = lax.dot_general(
        stack,
        jnp.where((target == wanted) & (source < 12), 1.0, 0.0),
        TN_DIMS,
        precision=lax.Precision.HIGHEST,
        preferred_element_type=f32,
    )
    spread = (st, sq)
    cut = lambda x: x.reshape(levels, high, lanes)
    flat = lambda i: rims[:, i * lanes : (i + 1) * lanes]
    w = weights(cut(gx[...]), cut(gy[...]))
    full = (levels, high, lanes)
    lane, at = iota(full, 2), iota(full, 1)
    for k, (ref, out, rim_ref) in enumerate(((gt, t_out, st), (gq, q_out, sq))):
        f = cut(ref[...])
        for step in range(2):
            rim_ref[step, 0] = flat((0, 4)[step] + k)
            if step == 0:
                rim_ref[step, 1] = flat(2 + k)
            tall_rim = ref
            for r in range(rows):
                tall_rim[pl.ds(pad + r, levels, stride=high), :] = rim_ref[step, 0, pl.ds(r, levels, stride=rows), :]
            if step == 0:
                tall_rim[pl.ds(pad - 1, levels, stride=high), :] = rim_ref[step, 1, pl.ds(0, levels, stride=rows), :]
                tall_rim[pl.ds(pad + rows, levels, stride=high), :] = rim_ref[
                    step, 1, pl.ds(rows - 1, levels, stride=rows), :
                ]
            rim = cut(tall_rim[...])
            e = jnp.where(lane == lanes - 1, rim, pltpu.roll(f, lanes - 1, 2))
            wst = jnp.where(lane == 0, rim, pltpu.roll(f, 1, 2))
            n = jnp.where(last & (at == pad + rows - 1), f, pltpu.roll(f, high - 1, 1))
            s = jnp.where(first & (at == pad), f, pltpu.roll(f, 1, 1))
            f = blend(w, f, e, wst, n, s)
        ref[...] = f.reshape(levels * high, lanes)
        for r in range(rows):
            out[pl.ds(r, levels, stride=rows), :] = ref[pl.ds(pad + r, levels, stride=high), :]


def advect(ft, fq, fx, fy, edges, lat_a, lat_b, lon_a, lon_b, rows, pad):
    tall, lanes = ft.shape
    total = edges.shape[1]
    grid = pltpu.VMEM((tall, lanes), f32)
    return pl.pallas_call(
        functools.partial(advect_kernel, rows, pad),
        out_shape=(shape_of(total, lanes), shape_of(total, lanes)),
        in_specs=[VMEM_SPEC] * 9,
        out_specs=(VMEM_SPEC,) * 2,
        scratch_shapes=[grid] * 4 + [pltpu.VMEM((2, 2, total, lanes), f32)] * 2,
        name="advect",
    )(*held(ft, fq, fx, fy, edges, lat_a, lat_b, lon_a, lon_b))

SLOTS, AHEAD = 16, 8


def heating_kernel(
    factor, linear, tables, masks, shares, albedos, scale, out, trans, pull, beam, total
):
    gpoints, levels = shares.shape
    rows, lanes = scale.shape
    wide = 2 * lanes
    engines = rows // 2
    total[...] = jnp.zeros_like(total)
    units = [(a, b) for a in range(2) for b in range(rows)]
    each = range(len(units))

    def main(*sums):
        def at(m, l):
            return sums[m * SLOTS + l % SLOTS]

        def group(i):
            start = pl.multiple_of(i * 16, 16)
            starts = [pl.multiple_of(start + 8 * a, 8) for a in range(2)]
            plain, absorbing = (tables[j, pl.ds(start, 16), :] for j in range(2))
            w15 = [albedos[pl.ds(s, 8), :] for s in starts]
            share = [shares[pl.ds(s, 8), :] for s in starts]
            blank = jnp.zeros((16, lanes), bf16)

            def issue(l):
                stack = [
                    jnp.concatenate([plain * masks[0, l], blank], axis=1),
                    jnp.concatenate([absorbing * masks[1, l], blank], axis=1),
                    jnp.concatenate([blank, plain * masks[2, l]], axis=1),
                ]
                stack = jnp.concatenate(stack, axis=0)
                for m in range(engines):
                    pltpu.matmul_acc_lhs(at(m, l), stack)

            for l in range(AHEAD):
                issue(l)
            y = current = step = None
            for l in range(levels):
                if l + AHEAD < levels:
                    issue(l + AHEAD)
                popped = [pltpu.matmul_pop(at(m, l)) for m in range(engines)]

                def part(kind, a, b):
                    s = kind * 16 + a * 8
                    return popped[b // 2][s : s + 8, (b % 2) * lanes : (b % 2 + 1) * lanes]

                resist, shunt, path = ([part(i, a, b) for a, b in units] for i in range(3))
                direct = [jnp.exp2(p) for p in path]
                source = [w15[units[u][0]] * direct[u] for u in each]
                for u in each:
                    beam[u, l] = direct[u]
                if l == 0:
                    y, current = shunt, source
                else:
                    y = [shunt[u] + y[u] * step[u] for u in each]
                    current = [source[u] + current[u] * step[u] for u in each]
                if l < levels - 1:
                    step = [1.0 / (1.0 + resist[u] * y[u]) for u in each]
                    for u in each:
                        trans[u, l] = step[u]
                        pull[u, l] = resist[u] * current[u]
            diffuse = [current[u] / y[u] for u in each]
            for l in range(levels - 1, -1, -1):
                if l < levels - 1:
                    diffuse = [trans[u, l] * (pull[u, l] + diffuse[u]) for u in each]
                spread = [jnp.broadcast_to(share[a][:, l : l + 1], (8, lanes)) for a in range(2)]
                for b in range(rows):
                    pair = [
                        (diffuse[a * rows + b] + beam[a * rows + b, l]) * spread[a]
                        for a in range(2)
                    ]
                    total[l, b] = total[l, b] + (pair[0] + pair[1])

        nothing = jnp.zeros((16, wide), bf16)
        for m in range(engines):
            last = sums[engines * SLOTS + m]
            pltpu.matmul_push_rhs(linear[:, m * wide : (m + 1) * wide], 0, m)
            pltpu.matmul_acc_lhs(last, nothing, load_staged_rhs=0)
            pltpu.matmul_pop(last)
        pl.loop(0, gpoints // 16)(group)

    pl.run_scoped(
        main,
        *[pltpu.ACC(m)((48, wide), f32) for m in range(engines) for _ in range(SLOTS)],
        *[pltpu.ACC(m)((16, wide), f32) for m in range(engines)],
    )
    column_scale = scale[...]
    for l in range(levels):
        here = pl.ds(l * rows, rows)
        out[here, :] = jnp.sum(total[l], axis=1) * column_scale * factor[here, :]


def heating(factor, linear, tables, masks, shares, albedos, scale):
    rows, lanes = scale.shape
    gpoints, levels = shares.shape
    stage = pltpu.VMEM((2 * rows, levels, 8, lanes), f32)
    cells = gpoints * levels * rows * lanes
    return pl.pallas_call(
        heating_kernel,
        out_shape=shape_of(levels * rows, lanes),
        in_specs=[VMEM_SPEC] * 7,
        out_specs=VMEM_SPEC,
        scratch_shapes=[stage, stage, stage, pltpu.VMEM((levels, rows, 8, lanes), f32)],
        cost_estimate=pl.CostEstimate(flops=640 * cells, bytes_accessed=1 << 20, transcendentals=2 * cells),
        name="heating",
    )(*held(factor, linear, tables, masks, shares, albedos, scale))

def local(
    thermal_deviation,
    moisture_deviation,
    eastward_stability,
    northward_stability,
    sun_height_ratio,
    extinction_coeff,
    reflectivity_ratio,
    insolation_source,
    daylight_tally,
    daylight_permutation,
):
    levels, rows, lanes = thermal_deviation.shape
    pad = 2
    lat_count, lon_count = lax.axis_size("lat"), lax.axis_size("lon")
    flat = lambda x: x.reshape(levels * rows, lanes)
    t, q, cx, cy = (
        flat(x)
        for x in (thermal_deviation, moisture_deviation, eastward_stability, northward_stability)
    )
    to_a, to_b = edge_rows(t, q, cx, cy, rows)
    lat_b = lax.ppermute(to_b, "lat", swaps(lat_count, 1, False))
    lat_a = lax.ppermute(to_a, "lat", swaps(lat_count, 0, False))
    *tables, ft, fq, fx, fy, own = prepare(
        t,
        q,
        cx,
        cy,
        sun_height_ratio,
        jnp.transpose(extinction_coeff),
        reflectivity_ratio.reshape(1, -1),
        insolation_source.reshape(1, -1),
        daylight_tally,
        daylight_permutation,
        pad,
    )
    edges, to_a, to_b = edge_columns(ft, fq, own, lat_a, lat_b, rows, pad)
    lon_b = lax.ppermute(to_b, "lon", swaps(lon_count, 1, True))
    lon_a = lax.ppermute(to_a, "lon", swaps(lon_count, 0, True))
    warming = heating(*tables)
    t_next, q_next = advect(ft, fq, fx, fy, edges, lat_a, lat_b, lon_a, lon_b, rows, pad)
    whole = lambda x: x.reshape(levels, rows, lanes)
    return whole(t_next), whole(q_next), whole(warming)


def solution(mesh):
    volume, surface = P(None, "lat", "lon"), P("lat", "lon")
    placed = (volume,) * 4 + (surface, P(), P(), P(), surface, P("lat", "lon", None))
    step = jax.shard_map(
        local, mesh=mesh, in_specs=placed, out_specs=(volume,) * 3, check_vma=False
    )
    return step
```

```python
import functools
import math

import jax
import jax.numpy as jnp
import ml_dtypes
import numpy as np
from jax import lax
from jax.experimental import pallas as pl
from jax.experimental.pallas import tpu as pltpu
from jax.sharding import PartitionSpec as P

heat_coeff = 20.0
f32, bf16 = jnp.float32, jnp.bfloat16
HELD = pltpu.VMEM
VMEM_SPEC = pl.BlockSpec(memory_space=pltpu.VMEM)
SMEM_SPEC = pl.BlockSpec(memory_space=pltpu.SMEM)
NT_DIMS = (((1,), (1,)), ((), ()))
TN_DIMS = (((0,), (0,)), ((), ()))


def iota(shape, dim):
    return lax.broadcasted_iota(jnp.int32, shape, dim)


def shape_of(*dims):
    return jax.ShapeDtypeStruct(dims, f32)


def held(*arrays):
    return [pltpu.with_memory_space_constraint(x, pltpu.VMEM) for x in arrays]


def swaps(count, first, ring):
    pairs = []
    for i in range(first, count, 2):
        j = i + 1
        if j == count and not ring:
            break
        pairs += [(i, j % count), (j % count, i)]
    return pairs


def odd_swaps(lat_count, lon_count):
    pairs = []
    for lon in range(lon_count):
        pairs += [(lon * lat_count + i, lon * lat_count + j) for i, j in swaps(lat_count, 1, False)]
        beside = lon + 1 if lon % 2 == 0 else lon - 1
        ends = {0} | ({lat_count - 1} if lat_count % 2 == 0 else set())
        pairs += [(lon * lat_count + end, beside * lat_count + end) for end in sorted(ends)]
    return pairs


def put_rows(blocks, rows, high_side, out):
    levels = blocks[0].shape[0] // rows
    t, q, cx, cy = blocks
    for k, (ref, deep) in enumerate(((t, 0), (t, 1), (q, 0), (q, 1), (cx, 0), (cy, 0))):
        high, low = (ref[pl.ds(r, levels, stride=rows), :] for r in (rows - 1 - deep, deep))
        out[k * levels : (k + 1) * levels, :] = jnp.where(high_side, high, low)


def rows_kernel(rows, t, q, cx, cy, to_a):
    put_rows((t, q, cx, cy), rows, lax.rem(lax.axis_index("lat"), 2) == 0, to_a)


def edge_rows(t, q, cx, cy, rows):
    total, lanes = t.shape
    return pl.pallas_call(
        functools.partial(rows_kernel, rows),
        out_shape=HELD((6 * (total // rows), lanes), f32),
        in_specs=[VMEM_SPEC] * 4,
        out_specs=VMEM_SPEC,
        name="edge_rows",
    )(t, q, cx, cy)


def halves(x):
    high = x.astype(bf16)
    return high, (x - high.astype(f32)).astype(bf16)


def thirds(value):
    left, parts = np.float32(value), []
    for _ in range(3):
        part = np.float32(left.astype(ml_dtypes.bfloat16))
        parts.append(float(part))
        left = np.float32(left - part)
    return parts


def pick_edges(slots, lanes, blocks):
    which, lane = iota((16, lanes), 0), iota((16, lanes), 1)
    edges = None
    for block, at in zip(blocks, slots):
        pick = jnp.zeros((16, lanes), jnp.bool_)
        for deep, k in enumerate(at):
            pick |= (which == k) & (lane == lanes - 1 - deep)
            pick |= (which == 8 + k) & (lane == deep)
        part = lax.dot_general(
            jnp.where(pick, 1.0, 0.0),
            block,
            NT_DIMS,
            precision=lax.Precision.HIGHEST,
            preferred_element_type=f32,
        )
        edges = part if edges is None else edges + part
    return edges


def prepare_kernel(
    pad, t, q, cx, cy, mu, k, albedo, solar, tally, perm,
    to_b, factor, linear, tables, masks, shares, albedos, scale, ft, fq, fx, fy, own,
):
    levels, gpoints = k.shape
    rows, lanes = mu.shape
    tall = rows + 2 * pad
    blocks = (t, q, cx, cy)
    put_rows(blocks, rows, lax.rem(lax.axis_index("lat"), 2) == 1, to_b)
    for ref, out in zip(blocks, (ft, fq, fx, fy)):
        for r in range(rows):
            out[pl.ds(pad + r, levels, stride=tall), :] = ref[pl.ds(r, levels, stride=rows), :]
    own[...] = pick_edges(((0, 1), (2, 3), (4,), (5,)), lanes, [ref[...] for ref in blocks])

    count = tally[0, 0]
    found = jnp.zeros((8, lanes), f32)
    for r in range(rows):
        column = perm[0, :, r * lanes : (r + 1) * lanes]
        row_at = column // lanes
        lane_at = column - row_at * lanes
        sunlit = iota((1, lanes), 1) + r * lanes < count
        at_row = jnp.where((row_at == iota((8, lanes), 0)) & sunlit, 1.0, 0.0).astype(bf16)
        at_lane = jnp.where(lane_at == iota((lanes, lanes), 0), 1.0, 0.0).astype(bf16)
        found += lax.dot_general(at_row, at_lane, NT_DIMS, preferred_element_type=f32)
    scale[...] = heat_coeff * mu[...] * found[:rows]

    quarter = lanes // 4
    factor[...] = (1.5 + jnp.tanh(q[...])) * (1.0 + 0.25 * jnp.tanh(t[...]))
    ones = jnp.ones((quarter, lanes), bf16)
    for r in range(rows):
        level_factor = factor[pl.ds(r, levels, stride=rows), :]
        per_path = level_factor * (-math.log2(math.e) / mu[r : r + 1, :])
        for start, value in ((0, level_factor), (lanes, per_path)):
            high, low = halves(value)
            linear[start : start + lanes, r * lanes : (r + 1) * lanes] = jnp.concatenate(
                [high, high, low, ones], axis=0
            )
    square = iota((gpoints, gpoints), 0) == iota((gpoints, gpoints), 1)

    def upright(row):
        return jnp.sum(jnp.where(square, row, 0.0), axis=1, keepdims=True)

    w = upright(albedo[...])
    filled = jnp.concatenate([k[...], jnp.zeros((levels, lanes - gpoints), f32)], axis=1)
    coeff = jnp.transpose(filled)[:gpoints]
    slot = iota((1, quarter), 1)

    def table(value, constants):
        high = value.astype(bf16).astype(f32)
        tail = jnp.zeros((1, quarter), f32)
        for i, c in enumerate(constants):
            tail = jnp.where(slot == i, c, tail)
        tail = jnp.broadcast_to(tail, (gpoints, quarter))
        return jnp.concatenate([high, value - high, high, tail], axis=1).astype(bf16)

    tables[0] = table(coeff, thirds(1.0 / 3.0))
    tables[1] = table(1.5 * (1.0 - w) * coeff, (0.75,))
    shares[...] = (1.0 - w) * upright(solar[...]) * coeff
    albedos[...] = jnp.broadcast_to(1.5 * w, (gpoints, lanes))
    lane = iota((16, lanes), 1)
    level, constant = lax.rem(lane, quarter), lane >= 3 * quarter
    for l in range(levels):
        masks[0, l] = jnp.where(constant | (level == l) | (level == l + 1), 1.0, 0.0).astype(bf16)
        masks[1, l] = jnp.where(constant | (level == l), 1.0, 0.0).astype(bf16)
        masks[2, l] = jnp.where(
            constant, 0.0, jnp.where(level < l, 1.0, jnp.where(level == l, 0.5, 0.0))
        ).astype(bf16)


def prepare(t, q, cx, cy, mu, k, albedo, solar, tally, perm, pad):
    levels, gpoints = k.shape
    rows, lanes = mu.shape
    tall = levels * (rows + 2 * pad)
    return pl.pallas_call(
        functools.partial(prepare_kernel, pad),
        out_shape=(
            HELD((6 * levels, lanes), f32),
            HELD(t.shape, f32),
            HELD((2 * lanes, rows * lanes), bf16),
            HELD((2, gpoints, lanes), bf16),
            HELD((3, levels, 16, lanes), bf16),
            HELD((gpoints, levels), f32),
            HELD((gpoints, lanes), f32),
            HELD((rows, lanes), f32),
            *[HELD((tall, lanes), f32)] * 4,
            HELD((16, levels * rows), f32),
        ),
        in_specs=[VMEM_SPEC] * 8 + [SMEM_SPEC, VMEM_SPEC],
        out_specs=(VMEM_SPEC,) * 13,
        cost_estimate=pl.CostEstimate(flops=1 << 22, bytes_accessed=1 << 21, transcendentals=1 << 17),
        name="prepare",
    )(t, q, cx, cy, mu, k, albedo, solar, tally, perm)


def by_side(even, first, last, from_a, from_b, k, levels, low, high):
    a, b = from_a[k * levels : (k + 1) * levels, :], from_b[k * levels : (k + 1) * levels, :]
    south, north = jnp.where(even, b, a), jnp.where(even, a, b)
    return jnp.where(first, low, south), jnp.where(last, high, north)


def lat_place():
    lat = lax.axis_index("lat")
    return lax.rem(lat, 2) == 0, lat == 0, lat == lax.axis_size("lat") - 1


def columns_kernel(pad, ft, fq, own, from_a, from_b, _, edges, to_a, to_b, ring):
    levels = from_a.shape[0] // 6
    total, lanes = ring.shape[1:]
    rows = total // levels
    tall = rows + 2 * pad
    ring[...] = jnp.zeros_like(ring)
    for i, ref in enumerate((ft, fq)):
        low, high = (ref[pl.ds(pad + r, levels, stride=tall), :] for r in (0, rows - 1))
        south, north = by_side(*lat_place(), from_a, from_b, 2 * i, levels, low, high)
        ring[i, pl.ds(0, levels, stride=rows), :] = south
        ring[i, pl.ds(rows - 1, levels, stride=rows), :] = north
    both = own[...] + pick_edges(((6,), (7,)), lanes, [ring[0], ring[1]])
    edges[...] = both
    even_lon = lax.rem(lax.axis_index("lon"), 2) == 0
    east, west = both[:8], both[8:]
    to_a[...] = jnp.where(even_lon, east, west)
    to_b[...] = jnp.where(even_lon, west, east)


def edge_columns(ft, fq, own, from_a, from_b, after, rows, pad):
    lanes = ft.shape[1]
    total = own.shape[1]
    return pl.pallas_call(
        functools.partial(columns_kernel, pad),
        out_shape=(HELD((16, total), f32), HELD((8, total), f32), HELD((8, total), f32)),
        in_specs=[VMEM_SPEC] * 6,
        out_specs=(VMEM_SPEC,) * 3,
        scratch_shapes=[pltpu.VMEM((2, total, lanes), f32)],
        name="edge_columns",
    )(*held(ft, fq, own, from_a, from_b, after))


def weights(cx, cy):
    hx, hy = 0.5 * cx, 0.5 * cy
    sx, sy = hx * cx, hy * cy
    return 1.0 - 2.0 * (sx + sy), sx - hx, sx + hx, sy - hy, sy + hy


def blend(w, here, east, west, north, south):
    return w[0] * here + w[1] * east + w[2] * west + w[3] * north + w[4] * south


def advect_kernel(
    rows, pad, ft, fq, fx, fy, edges, lat_a, lat_b, lon_a, lon_b, t_out, q_out, gt, gq, gx, gy, st, sq
):
    lanes = ft.shape[1]
    high = rows + 2 * pad
    levels = ft.shape[0] // high
    total = levels * rows
    place = lat_place()
    _, first, last = place
    grids = (gt, gq, gx, gy)
    for ref, grid, at in zip((ft, fq, fx, fy), grids, ((0, 1), (2, 3), (4,), (5,))):
        grid[...] = ref[...]
        low, top = (ref[pl.ds(pad + r, levels, stride=high), :] for r in (0, rows - 1))
        for deep in range(pad):
            k = at[min(deep, len(at) - 1)]
            south, north = by_side(*place, lat_a, lat_b, k, levels, low, top)
            grid[pl.ds(pad - 1 - deep, levels, stride=high), :] = south
            grid[pl.ds(pad + rows + deep, levels, stride=high), :] = north
    even_lon = lax.rem(lax.axis_index("lon"), 2) == 0
    a, b = lon_a[...], lon_b[...]
    east, west = jnp.where(even_lon, a, b), jnp.where(even_lon, b, a)
    mine = edges[...]

    def strip(x, k):
        return x[k : k + 1, :]

    row_of = lax.rem(iota((1, total), 1), rows)

    def up(x, k):
        return jnp.where(row_of == rows - 1, strip(x, 6 + k // 2), pltpu.roll(strip(x, k), total - 1, 1))

    def down(x, k):
        return jnp.where(row_of == 0, strip(x, 6 + k // 2), pltpu.roll(strip(x, k), 1, 1))

    ww = weights(strip(west, 4), strip(west, 5))
    we = weights(strip(east, 4), strip(east, 5))
    firsts = []
    for k in (0, 2):
        firsts.append(blend(ww, strip(west, k), strip(mine, 8 + k), strip(west, k + 1), up(west, k), down(west, k)))
        firsts.append(blend(we, strip(east, k), strip(east, k + 1), strip(mine, k), up(east, k), down(east, k)))
    stack = jnp.concatenate(
        [strip(x, k) for k in (0, 2, 6, 7) for x in (west, east)] + firsts + [jnp.zeros((4, total), f32)],
        axis=0,
    )
    source, target = iota((16, 6 * lanes), 0), iota((16, 6 * lanes), 1)
    wanted = (source // 2) * lanes + lax.rem(source, 2) * (lanes - 1)
    rims = lax.dot_general(
        stack,
        jnp.where((target == wanted) & (source < 12), 1.0, 0.0),
        TN_DIMS,
        precision=lax.Precision.HIGHEST,
        preferred_element_type=f32,
    )
    spread = (st, sq)
    cut = lambda x: x.reshape(levels, high, lanes)
    flat = lambda i: rims[:, i * lanes : (i + 1) * lanes]
    w = weights(cut(gx[...]), cut(gy[...]))
    full = (levels, high, lanes)
    lane, at = iota(full, 2), iota(full, 1)
    for k, (ref, out, rim_ref) in enumerate(((gt, t_out, st), (gq, q_out, sq))):
        f = cut(ref[...])
        for step in range(2):
            rim_ref[step, 0] = flat((0, 4)[step] + k)
            if step == 0:
                rim_ref[step, 1] = flat(2 + k)
            tall_rim = ref
            for r in range(rows):
                tall_rim[pl.ds(pad + r, levels, stride=high), :] = rim_ref[step, 0, pl.ds(r, levels, stride=rows), :]
            if step == 0:
                tall_rim[pl.ds(pad - 1, levels, stride=high), :] = rim_ref[step, 1, pl.ds(0, levels, stride=rows), :]
                tall_rim[pl.ds(pad + rows, levels, stride=high), :] = rim_ref[
                    step, 1, pl.ds(rows - 1, levels, stride=rows), :
                ]
            rim = cut(tall_rim[...])
            e = jnp.where(lane == lanes - 1, rim, pltpu.roll(f, lanes - 1, 2))
            wst = jnp.where(lane == 0, rim, pltpu.roll(f, 1, 2))
            n = jnp.where(last & (at == pad + rows - 1), f, pltpu.roll(f, high - 1, 1))
            s = jnp.where(first & (at == pad), f, pltpu.roll(f, 1, 1))
            f = blend(w, f, e, wst, n, s)
        ref[...] = f.reshape(levels * high, lanes)
        for r in range(rows):
            out[pl.ds(r, levels, stride=rows), :] = ref[pl.ds(pad + r, levels, stride=high), :]


def advect(ft, fq, fx, fy, edges, lat_a, lat_b, lon_a, lon_b, rows, pad):
    tall, lanes = ft.shape
    total = edges.shape[1]
    grid = pltpu.VMEM((tall, lanes), f32)
    return pl.pallas_call(
        functools.partial(advect_kernel, rows, pad),
        out_shape=(shape_of(total, lanes), shape_of(total, lanes)),
        in_specs=[VMEM_SPEC] * 9,
        out_specs=(VMEM_SPEC,) * 2,
        scratch_shapes=[grid] * 4 + [pltpu.VMEM((2, 2, total, lanes), f32)] * 2,
        name="advect",
    )(*held(ft, fq, fx, fy, edges, lat_a, lat_b, lon_a, lon_b))

SLOTS, AHEAD = 16, 8
EARLY = 5


def heating_kernel(
    begin, end, linear, tables, masks, shares, albedos, *refs
):
    gpoints, levels = shares.shape
    lanes = albedos.shape[1]
    rows = linear.shape[1] // lanes
    if begin == 0:
        total, trans, pull, beam = refs
    else:
        so_far, factor, scale, _, out, trans, pull, beam, total = refs
    wide = 2 * lanes
    engines = rows // 2
    total[...] = jnp.zeros_like(total) if begin == 0 else so_far[...]
    units = [(a, b) for a in range(2) for b in range(rows)]
    each = range(len(units))

    def main(*sums):
        def at(m, l):
            return sums[m * SLOTS + l % SLOTS]

        def group(i):
            start = pl.multiple_of(i * 16, 16)
            starts = [pl.multiple_of(start + 8 * a, 8) for a in range(2)]
            plain, absorbing = (tables[j, pl.ds(start, 16), :] for j in range(2))
            w15 = [albedos[pl.ds(s, 8), :] for s in starts]
            share = [shares[pl.ds(s, 8), :] for s in starts]
            blank = jnp.zeros((16, lanes), bf16)

            def issue(l):
                stack = [
                    jnp.concatenate([plain * masks[0, l], blank], axis=1),
                    jnp.concatenate([absorbing * masks[1, l], blank], axis=1),
                    jnp.concatenate([blank, plain * masks[2, l]], axis=1),
                ]
                stack = jnp.concatenate(stack, axis=0)
                for m in range(engines):
                    pltpu.matmul_acc_lhs(at(m, l), stack)

            for l in range(AHEAD):
                issue(l)
            y = current = step = None
            for l in range(levels):
                if l + AHEAD < levels:
                    issue(l + AHEAD)
                popped = [pltpu.matmul_pop(at(m, l)) for m in range(engines)]

                def part(kind, a, b):
                    s = kind * 16 + a * 8
                    return popped[b // 2][s : s + 8, (b % 2) * lanes : (b % 2 + 1) * lanes]

                resist, shunt, path = ([part(i, a, b) for a, b in units] for i in range(3))
                direct = [jnp.exp2(p) for p in path]
                source = [w15[units[u][0]] * direct[u] for u in each]
                for u in each:
                    beam[u, l] = direct[u]
                if l == 0:
                    y, current = shunt, source
                else:
                    y = [shunt[u] + y[u] * step[u] for u in each]
                    current = [source[u] + current[u] * step[u] for u in each]
                if l < levels - 1:
                    step = [1.0 / (1.0 + resist[u] * y[u]) for u in each]
                    for u in each:
                        trans[u, l] = step[u]
                        pull[u, l] = resist[u] * current[u]
            diffuse = [current[u] / y[u] for u in each]
            for l in range(levels - 1, -1, -1):
                if l < levels - 1:
                    diffuse = [trans[u, l] * (pull[u, l] + diffuse[u]) for u in each]
                spread = [jnp.broadcast_to(share[a][:, l : l + 1], (8, lanes)) for a in range(2)]
                for b in range(rows):
                    pair = [
                        (diffuse[a * rows + b] + beam[a * rows + b, l]) * spread[a]
                        for a in range(2)
                    ]
                    total[l, b] = total[l, b] + (pair[0] + pair[1])

        nothing = jnp.zeros((16, wide), bf16)
        for m in range(engines):
            last = sums[engines * SLOTS + m]
            pltpu.matmul_push_rhs(linear[:, m * wide : (m + 1) * wide], 0, m)
            pltpu.matmul_acc_lhs(last, nothing, load_staged_rhs=0)
            pltpu.matmul_pop(last)
        pl.loop(begin, end)(group)

    pl.run_scoped(
        main,
        *[pltpu.ACC(m)((48, wide), f32) for m in range(engines) for _ in range(SLOTS)],
        *[pltpu.ACC(m)((16, wide), f32) for m in range(engines)],
    )
    if begin == 0:
        return
    column_scale = scale[...]
    for l in range(levels):
        here = pl.ds(l * rows, rows)
        out[here, :] = jnp.sum(total[l], axis=1) * column_scale * factor[here, :]


def heating(linear, tables, masks, shares, albedos, begin, end, more=()):
    gpoints, levels = shares.shape
    lanes = albedos.shape[1]
    rows = linear.shape[1] // lanes
    stage = pltpu.VMEM((2 * rows, levels, 8, lanes), f32)
    sums = (levels, rows, 8, lanes)
    cells = (end - begin) * 16 * levels * rows * lanes
    return pl.pallas_call(
        functools.partial(heating_kernel, begin, end),
        out_shape=shape_of(levels * rows, lanes) if more else HELD(sums, f32),
        in_specs=[VMEM_SPEC] * (5 + len(more)),
        out_specs=VMEM_SPEC,
        scratch_shapes=[stage, stage, stage] + [pltpu.VMEM(sums, f32)] * bool(more),
        cost_estimate=pl.CostEstimate(flops=640 * cells, bytes_accessed=1 << 20, transcendentals=2 * cells),
        name="heating",
    )(*held(linear, tables, masks, shares, albedos, *more))


def local(
    thermal_deviation,
    moisture_deviation,
    eastward_stability,
    northward_stability,
    sun_height_ratio,
    extinction_coeff,
    reflectivity_ratio,
    insolation_source,
    daylight_tally,
    daylight_permutation,
):
    levels, rows, lanes = thermal_deviation.shape
    pad = 2
    lat_count, lon_count = lax.axis_size("lat"), lax.axis_size("lon")
    flat = lambda x: x.reshape(levels * rows, lanes)
    t, q, cx, cy = (
        flat(x)
        for x in (thermal_deviation, moisture_deviation, eastward_stability, northward_stability)
    )
    to_a = edge_rows(t, q, cx, cy, rows)
    lat_a = lax.ppermute(to_a, "lat", swaps(lat_count, 0, False))
    to_b, factor, *tables, scale, ft, fq, fx, fy, own = prepare(
        t,
        q,
        cx,
        cy,
        sun_height_ratio,
        jnp.transpose(extinction_coeff),
        reflectivity_ratio.reshape(1, -1),
        insolation_source.reshape(1, -1),
        daylight_tally,
        daylight_permutation,
        pad,
    )
    lat_b = lax.ppermute(to_b, ("lon", "lat"), odd_swaps(lat_count, lon_count))
    groups = extinction_coeff.shape[0] // 16
    early = min(EARLY, groups - 1)
    sums = heating(*tables, 0, early)
    edges, to_a, to_b = edge_columns(ft, fq, own, lat_a, lat_b, sums, rows, pad)
    lon_b = lax.ppermute(to_b, "lon", swaps(lon_count, 1, True))
    lon_a = lax.ppermute(to_a, "lon", swaps(lon_count, 0, True))
    warming = heating(*tables, early, groups, (sums, factor, scale, edges))
    t_next, q_next = advect(ft, fq, fx, fy, edges, lat_a, lat_b, lon_a, lon_b, rows, pad)
    whole = lambda x: x.reshape(levels, rows, lanes)
    return whole(t_next), whole(q_next), whole(warming)


def solution(mesh):
    volume, surface = P(None, "lat", "lon"), P("lat", "lon")
    placed = (volume,) * 4 + (surface, P(), P(), P(), surface, P("lat", "lon", None))
    step = jax.shard_map(
        local, mesh=mesh, in_specs=placed, out_specs=(volume,) * 3, check_vma=False
    )
    return step
```

```python
import functools
import math

import jax
import jax.numpy as jnp
import ml_dtypes
import numpy as np
from jax import lax
from jax.experimental import pallas as pl
from jax.experimental.pallas import tpu as pltpu
from jax.sharding import PartitionSpec as P

heat_coeff = 20.0
f32, bf16 = jnp.float32, jnp.bfloat16
HELD = pltpu.VMEM
VMEM_SPEC = pl.BlockSpec(memory_space=pltpu.VMEM)
SMEM_SPEC = pl.BlockSpec(memory_space=pltpu.SMEM)
NT_DIMS = (((1,), (1,)), ((), ()))
TN_DIMS = (((0,), (0,)), ((), ()))


def iota(shape, dim):
    return lax.broadcasted_iota(jnp.int32, shape, dim)


def shape_of(*dims):
    return jax.ShapeDtypeStruct(dims, f32)


def held(*arrays):
    return [pltpu.with_memory_space_constraint(x, pltpu.VMEM) for x in arrays]


def swaps(count, first, ring):
    pairs = []
    for i in range(first, count, 2):
        j = i + 1
        if j == count and not ring:
            break
        pairs += [(i, j % count), (j % count, i)]
    return pairs


def odd_swaps(lat_count, lon_count):
    pairs = []
    for lon in range(lon_count):
        pairs += [(lon * lat_count + i, lon * lat_count + j) for i, j in swaps(lat_count, 1, False)]
        beside = lon + 1 if lon % 2 == 0 else lon - 1
        ends = {0} | ({lat_count - 1} if lat_count % 2 == 0 else set())
        pairs += [(lon * lat_count + end, beside * lat_count + end) for end in sorted(ends)]
    return pairs


def put_rows(blocks, rows, high_side, out):
    levels = blocks[0].shape[0] // rows
    t, q, cx, cy = blocks
    for k, (ref, deep) in enumerate(((t, 0), (t, 1), (q, 0), (q, 1), (cx, 0), (cy, 0))):
        high, low = (ref[pl.ds(r, levels, stride=rows), :] for r in (rows - 1 - deep, deep))
        out[k * levels : (k + 1) * levels, :] = jnp.where(high_side, high, low)


def rows_kernel(rows, tally, perm, *refs):
    count = (len(refs) - 3) // 2
    inputs, (to_a, to_b, sunlit), copies = refs[:count], refs[count : count + 3], refs[count + 3 :]
    even = lax.rem(lax.axis_index("lat"), 2) == 0
    put_rows(inputs[:4], rows, even, to_a)
    put_rows(inputs[:4], rows, jnp.logical_not(even), to_b)
    sunlit[...] = jnp.where(iota(perm.shape, 2) < tally[0, 0], perm[...], -1)
    for ref, copy in zip(inputs, copies):
        copy[...] = ref[...]


def edge_rows(rows, tally, perm, *arrays):
    total, lanes = arrays[0].shape
    sent = HELD((6 * (total // rows), lanes), f32)
    to_a, to_b, sunlit, *copies = pl.pallas_call(
        functools.partial(rows_kernel, rows),
        out_shape=(sent, sent, *(HELD(x.shape, x.dtype) for x in (perm, *arrays))),
        in_specs=[SMEM_SPEC] + [VMEM_SPEC] * (1 + len(arrays)),
        out_specs=(VMEM_SPEC,) * (3 + len(arrays)),
        name="edge_rows",
    )(tally, perm, *arrays)
    return to_a, to_b, (*copies, sunlit)


def halves(x):
    high = x.astype(bf16)
    return high, (x - high.astype(f32)).astype(bf16)


def thirds(value):
    left, parts = np.float32(value), []
    for _ in range(3):
        part = np.float32(left.astype(ml_dtypes.bfloat16))
        parts.append(float(part))
        left = np.float32(left - part)
    return parts


def pick_edges(slots, lanes, blocks):
    which, lane = iota((16, lanes), 0), iota((16, lanes), 1)
    edges = None
    for block, at in zip(blocks, slots):
        pick = jnp.zeros((16, lanes), jnp.bool_)
        for deep, k in enumerate(at):
            pick |= (which == k) & (lane == lanes - 1 - deep)
            pick |= (which == 8 + k) & (lane == deep)
        part = lax.dot_general(
            jnp.where(pick, 1.0, 0.0),
            block,
            NT_DIMS,
            precision=lax.Precision.HIGHEST,
            preferred_element_type=f32,
        )
        edges = part if edges is None else edges + part
    return edges


def prepare_kernel(
    pad, t, q, cx, cy, mu, k, albedo, solar, sunlit,
    factor, linear, tables, masks, shares, albedos, scale, ft, fq, fx, fy, own,
):
    levels, gpoints = k.shape
    rows, lanes = mu.shape
    tall = rows + 2 * pad
    blocks = (t, q, cx, cy)
    for ref, out in zip(blocks, (ft, fq, fx, fy)):
        for r in range(rows):
            out[pl.ds(pad + r, levels, stride=tall), :] = ref[pl.ds(r, levels, stride=rows), :]
    own[...] = pick_edges(((0, 1), (2, 3), (4,), (5,)), lanes, [ref[...] for ref in blocks])

    found = jnp.zeros((8, lanes), f32)
    for r in range(rows):
        column = sunlit[0, :, r * lanes : (r + 1) * lanes]
        row_at = jnp.where(column < 0, -1, column // lanes)
        lane_at = lax.rem(column, lanes)
        at_row = jnp.where(row_at == iota((8, lanes), 0), 1.0, 0.0).astype(bf16)
        at_lane = jnp.where(lane_at == iota((lanes, lanes), 0), 1.0, 0.0).astype(bf16)
        found += lax.dot_general(at_row, at_lane, NT_DIMS, preferred_element_type=f32)
    scale[...] = heat_coeff * mu[...] * found[:rows]

    quarter = lanes // 4
    factor[...] = (1.5 + jnp.tanh(q[...])) * (1.0 + 0.25 * jnp.tanh(t[...]))
    ones = jnp.ones((quarter, lanes), bf16)
    for r in range(rows):
        level_factor = factor[pl.ds(r, levels, stride=rows), :]
        per_path = level_factor * (-math.log2(math.e) / mu[r : r + 1, :])
        for start, value in ((0, level_factor), (lanes, per_path)):
            high, low = halves(value)
            linear[start : start + lanes, r * lanes : (r + 1) * lanes] = jnp.concatenate(
                [high, high, low, ones], axis=0
            )
    square = iota((gpoints, gpoints), 0) == iota((gpoints, gpoints), 1)

    def upright(row):
        return jnp.sum(jnp.where(square, row, 0.0), axis=1, keepdims=True)

    w = upright(albedo[...])
    filled = jnp.concatenate([k[...], jnp.zeros((levels, lanes - gpoints), f32)], axis=1)
    coeff = jnp.transpose(filled)[:gpoints]
    slot = iota((1, quarter), 1)

    def table(value, constants):
        high = value.astype(bf16).astype(f32)
        tail = jnp.zeros((1, quarter), f32)
        for i, c in enumerate(constants):
            tail = jnp.where(slot == i, c, tail)
        tail = jnp.broadcast_to(tail, (gpoints, quarter))
        return jnp.concatenate([high, value - high, high, tail], axis=1).astype(bf16)

    tables[0] = table(coeff, thirds(1.0 / 3.0))
    tables[1] = table(1.5 * (1.0 - w) * coeff, (0.75,))
    shares[...] = (1.0 - w) * upright(solar[...]) * coeff
    albedos[...] = jnp.broadcast_to(1.5 * w, (gpoints, lanes))
    lane = iota((16, lanes), 1)
    level, constant = lax.rem(lane, quarter), lane >= 3 * quarter
    for l in range(levels):
        masks[0, l] = jnp.where(constant | (level == l) | (level == l + 1), 1.0, 0.0).astype(bf16)
        masks[1, l] = jnp.where(constant | (level == l), 1.0, 0.0).astype(bf16)
        masks[2, l] = jnp.where(
            constant, 0.0, jnp.where(level < l, 1.0, jnp.where(level == l, 0.5, 0.0))
        ).astype(bf16)


def prepare(t, q, cx, cy, mu, k, albedo, solar, sunlit, pad):
    levels, gpoints = k.shape
    rows, lanes = mu.shape
    tall = levels * (rows + 2 * pad)
    return pl.pallas_call(
        functools.partial(prepare_kernel, pad),
        out_shape=(
            HELD(t.shape, f32),
            HELD((2 * lanes, rows * lanes), bf16),
            HELD((2, gpoints, lanes), bf16),
            HELD((3, levels, 16, lanes), bf16),
            HELD((gpoints, levels), f32),
            HELD((gpoints, lanes), f32),
            HELD((rows, lanes), f32),
            *[HELD((tall, lanes), f32)] * 4,
            HELD((16, levels * rows), f32),
        ),
        in_specs=[VMEM_SPEC] * 9,
        out_specs=(VMEM_SPEC,) * 12,
        cost_estimate=pl.CostEstimate(flops=1 << 22, bytes_accessed=1 << 21, transcendentals=1 << 17),
        name="prepare",
    )(*held(t, q, cx, cy, mu, k, albedo, solar, sunlit))


def by_side(even, first, last, from_a, from_b, k, levels, low, high):
    a, b = from_a[k * levels : (k + 1) * levels, :], from_b[k * levels : (k + 1) * levels, :]
    south, north = jnp.where(even, b, a), jnp.where(even, a, b)
    return jnp.where(first, low, south), jnp.where(last, high, north)


def lat_place():
    lat = lax.axis_index("lat")
    return lax.rem(lat, 2) == 0, lat == 0, lat == lax.axis_size("lat") - 1


def columns_kernel(pad, ft, fq, own, from_a, from_b, _, edges, to_a, to_b, ring):
    levels = from_a.shape[0] // 6
    total, lanes = ring.shape[1:]
    rows = total // levels
    tall = rows + 2 * pad
    ring[...] = jnp.zeros_like(ring)
    for i, ref in enumerate((ft, fq)):
        low, high = (ref[pl.ds(pad + r, levels, stride=tall), :] for r in (0, rows - 1))
        south, north = by_side(*lat_place(), from_a, from_b, 2 * i, levels, low, high)
        ring[i, pl.ds(0, levels, stride=rows), :] = south
        ring[i, pl.ds(rows - 1, levels, stride=rows), :] = north
    both = own[...] + pick_edges(((6,), (7,)), lanes, [ring[0], ring[1]])
    edges[...] = both
    even_lon = lax.rem(lax.axis_index("lon"), 2) == 0
    east, west = both[:8], both[8:]
    to_a[...] = jnp.where(even_lon, east, west)
    to_b[...] = jnp.where(even_lon, west, east)


def edge_columns(ft, fq, own, from_a, from_b, after, rows, pad):
    lanes = ft.shape[1]
    total = own.shape[1]
    return pl.pallas_call(
        functools.partial(columns_kernel, pad),
        out_shape=(HELD((16, total), f32), HELD((8, total), f32), HELD((8, total), f32)),
        in_specs=[VMEM_SPEC] * 6,
        out_specs=(VMEM_SPEC,) * 3,
        scratch_shapes=[pltpu.VMEM((2, total, lanes), f32)],
        name="edge_columns",
    )(*held(ft, fq, own, from_a, from_b, after))


def weights(cx, cy):
    hx, hy = 0.5 * cx, 0.5 * cy
    sx, sy = hx * cx, hy * cy
    return 1.0 - 2.0 * (sx + sy), sx - hx, sx + hx, sy - hy, sy + hy


def blend(w, here, east, west, north, south):
    return w[0] * here + w[1] * east + w[2] * west + w[3] * north + w[4] * south


def advect_kernel(
    rows, pad, ft, fq, fx, fy, edges, lat_a, lat_b, lon_a, lon_b, t_out, q_out, gt, gq, gx, gy, st, sq
):
    lanes = ft.shape[1]
    high = rows + 2 * pad
    levels = ft.shape[0] // high
    total = levels * rows
    place = lat_place()
    _, first, last = place
    grids = (gt, gq, gx, gy)
    for ref, grid, at in zip((ft, fq, fx, fy), grids, ((0, 1), (2, 3), (4,), (5,))):
        grid[...] = ref[...]
        low, top = (ref[pl.ds(pad + r, levels, stride=high), :] for r in (0, rows - 1))
        for deep in range(pad):
            k = at[min(deep, len(at) - 1)]
            south, north = by_side(*place, lat_a, lat_b, k, levels, low, top)
            grid[pl.ds(pad - 1 - deep, levels, stride=high), :] = south
            grid[pl.ds(pad + rows + deep, levels, stride=high), :] = north
    even_lon = lax.rem(lax.axis_index("lon"), 2) == 0
    a, b = lon_a[...], lon_b[...]
    east, west = jnp.where(even_lon, a, b), jnp.where(even_lon, b, a)
    mine = edges[...]

    def strip(x, k):
        return x[k : k + 1, :]

    row_of = lax.rem(iota((1, total), 1), rows)

    def up(x, k):
        return jnp.where(row_of == rows - 1, strip(x, 6 + k // 2), pltpu.roll(strip(x, k), total - 1, 1))

    def down(x, k):
        return jnp.where(row_of == 0, strip(x, 6 + k // 2), pltpu.roll(strip(x, k), 1, 1))

    ww = weights(strip(west, 4), strip(west, 5))
    we = weights(strip(east, 4), strip(east, 5))
    firsts = []
    for k in (0, 2):
        firsts.append(blend(ww, strip(west, k), strip(mine, 8 + k), strip(west, k + 1), up(west, k), down(west, k)))
        firsts.append(blend(we, strip(east, k), strip(east, k + 1), strip(mine, k), up(east, k), down(east, k)))
    stack = jnp.concatenate(
        [strip(x, k) for k in (0, 2, 6, 7) for x in (west, east)] + firsts + [jnp.zeros((4, total), f32)],
        axis=0,
    )
    source, target = iota((16, 6 * lanes), 0), iota((16, 6 * lanes), 1)
    wanted = (source // 2) * lanes + lax.rem(source, 2) * (lanes - 1)
    rims = lax.dot_general(
        stack,
        jnp.where((target == wanted) & (source < 12), 1.0, 0.0),
        TN_DIMS,
        precision=lax.Precision.HIGHEST,
        preferred_element_type=f32,
    )
    spread = (st, sq)
    cut = lambda x: x.reshape(levels, high, lanes)
    flat = lambda i: rims[:, i * lanes : (i + 1) * lanes]
    w = weights(cut(gx[...]), cut(gy[...]))
    full = (levels, high, lanes)
    lane, at = iota(full, 2), iota(full, 1)
    for k, (ref, out, rim_ref) in enumerate(((gt, t_out, st), (gq, q_out, sq))):
        f = cut(ref[...])
        for step in range(2):
            rim_ref[step, 0] = flat((0, 4)[step] + k)
            if step == 0:
                rim_ref[step, 1] = flat(2 + k)
            tall_rim = ref
            for r in range(rows):
                tall_rim[pl.ds(pad + r, levels, stride=high), :] = rim_ref[step, 0, pl.ds(r, levels, stride=rows), :]
            if step == 0:
                tall_rim[pl.ds(pad - 1, levels, stride=high), :] = rim_ref[step, 1, pl.ds(0, levels, stride=rows), :]
                tall_rim[pl.ds(pad + rows, levels, stride=high), :] = rim_ref[
                    step, 1, pl.ds(rows - 1, levels, stride=rows), :
                ]
            rim = cut(tall_rim[...])
            e = jnp.where(lane == lanes - 1, rim, pltpu.roll(f, lanes - 1, 2))
            wst = jnp.where(lane == 0, rim, pltpu.roll(f, 1, 2))
            n = jnp.where(last & (at == pad + rows - 1), f, pltpu.roll(f, high - 1, 1))
            s = jnp.where(first & (at == pad), f, pltpu.roll(f, 1, 1))
            f = blend(w, f, e, wst, n, s)
        ref[...] = f.reshape(levels * high, lanes)
        for r in range(rows):
            out[pl.ds(r, levels, stride=rows), :] = ref[pl.ds(pad + r, levels, stride=high), :]


def advect(ft, fq, fx, fy, edges, lat_a, lat_b, lon_a, lon_b, rows, pad):
    tall, lanes = ft.shape
    total = edges.shape[1]
    grid = pltpu.VMEM((tall, lanes), f32)
    return pl.pallas_call(
        functools.partial(advect_kernel, rows, pad),
        out_shape=(shape_of(total, lanes), shape_of(total, lanes)),
        in_specs=[VMEM_SPEC] * 9,
        out_specs=(VMEM_SPEC,) * 2,
        scratch_shapes=[grid] * 4 + [pltpu.VMEM((2, 2, total, lanes), f32)] * 2,
        name="advect",
    )(*held(ft, fq, fx, fy, edges, lat_a, lat_b, lon_a, lon_b))

SLOTS, AHEAD = 16, 8
EARLY = 5


def heating_kernel(
    begin, end, linear, tables, masks, shares, albedos, *refs
):
    gpoints, levels = shares.shape
    lanes = albedos.shape[1]
    rows = linear.shape[1] // lanes
    if begin == 0:
        total, trans, pull, beam = refs
    else:
        so_far, factor, scale, _, out, trans, pull, beam, total = refs
    wide = 2 * lanes
    engines = rows // 2
    total[...] = jnp.zeros_like(total) if begin == 0 else so_far[...]
    units = [(a, b) for a in range(2) for b in range(rows)]
    each = range(len(units))

    def main(*sums):
        def at(m, l):
            return sums[m * SLOTS + l % SLOTS]

        blank = jnp.zeros((16, lanes), bf16)

        def issue(i, l):
            start = pl.multiple_of(i * 16, 16)
            plain, absorbing = (tables[j, pl.ds(start, 16), :] for j in range(2))
            stack = [
                jnp.concatenate([plain * masks[0, l], blank], axis=1),
                jnp.concatenate([absorbing * masks[1, l], blank], axis=1),
                jnp.concatenate([blank, plain * masks[2, l]], axis=1),
            ]
            stack = jnp.concatenate(stack, axis=0)
            for m in range(engines):
                pltpu.matmul_acc_lhs(at(m, l), stack)

        def group(i):
            start = pl.multiple_of(i * 16, 16)
            starts = [pl.multiple_of(start + 8 * a, 8) for a in range(2)]
            w15 = [albedos[pl.ds(s, 8), :] for s in starts]
            share = [shares[pl.ds(s, 8), :] for s in starts]
            following = jnp.minimum(i + 1, end - 1)
            y = current = step = None
            for l in range(levels):
                if l + AHEAD < levels:
                    issue(i, l + AHEAD)
                popped = [pltpu.matmul_pop(at(m, l)) for m in range(engines)]

                def part(kind, a, b):
                    s = kind * 16 + a * 8
                    return popped[b // 2][s : s + 8, (b % 2) * lanes : (b % 2 + 1) * lanes]

                resist, shunt, path = ([part(i, a, b) for a, b in units] for i in range(3))
                direct = [jnp.exp2(p) for p in path]
                source = [w15[units[u][0]] * direct[u] for u in each]
                for u in each:
                    beam[u, l] = direct[u]
                if l == 0:
                    y, current = shunt, source
                else:
                    y = [shunt[u] + y[u] * step[u] for u in each]
                    current = [source[u] + current[u] * step[u] for u in each]
                if l < levels - 1:
                    step = [1.0 / (1.0 + resist[u] * y[u]) for u in each]
                    for u in each:
                        trans[u, l] = step[u]
                        pull[u, l] = resist[u] * current[u]
            diffuse = [current[u] / y[u] for u in each]
            for l in range(levels - 1, -1, -1):
                if levels - 1 - l < AHEAD:
                    issue(following, levels - 1 - l)
                if l < levels - 1:
                    diffuse = [trans[u, l] * (pull[u, l] + diffuse[u]) for u in each]
                spread = [jnp.broadcast_to(share[a][:, l : l + 1], (8, lanes)) for a in range(2)]
                for b in range(rows):
                    pair = [
                        (diffuse[a * rows + b] + beam[a * rows + b, l]) * spread[a]
                        for a in range(2)
                    ]
                    total[l, b] = total[l, b] + (pair[0] + pair[1])

        nothing = jnp.zeros((16, wide), bf16)
        for m in range(engines):
            last = sums[engines * SLOTS + m]
            pltpu.matmul_push_rhs(linear[:, m * wide : (m + 1) * wide], 0, m)
            pltpu.matmul_acc_lhs(last, nothing, load_staged_rhs=0)
            pltpu.matmul_pop(last)
        for l in range(AHEAD):
            issue(begin, l)
        pl.loop(begin, end)(group)
        for l in range(AHEAD):
            for m in range(engines):
                pltpu.matmul_pop(at(m, l))

    pl.run_scoped(
        main,
        *[pltpu.ACC(m)((48, wide), f32) for m in range(engines) for _ in range(SLOTS)],
        *[pltpu.ACC(m)((16, wide), f32) for m in range(engines)],
    )
    if begin == 0:
        return
    column_scale = scale[...]
    for l in range(levels):
        here = pl.ds(l * rows, rows)
        out[here, :] = jnp.sum(total[l], axis=1) * column_scale * factor[here, :]


def heating(linear, tables, masks, shares, albedos, begin, end, more=()):
    gpoints, levels = shares.shape
    lanes = albedos.shape[1]
    rows = linear.shape[1] // lanes
    stage = pltpu.VMEM((2 * rows, levels, 8, lanes), f32)
    sums = (levels, rows, 8, lanes)
    cells = (end - begin) * 16 * levels * rows * lanes
    return pl.pallas_call(
        functools.partial(heating_kernel, begin, end),
        out_shape=shape_of(levels * rows, lanes) if more else HELD(sums, f32),
        in_specs=[VMEM_SPEC] * (5 + len(more)),
        out_specs=VMEM_SPEC,
        scratch_shapes=[stage, stage, stage] + [pltpu.VMEM(sums, f32)] * bool(more),
        cost_estimate=pl.CostEstimate(flops=640 * cells, bytes_accessed=1 << 20, transcendentals=2 * cells),
        name="heating",
    )(*held(linear, tables, masks, shares, albedos, *more))


def local(
    thermal_deviation,
    moisture_deviation,
    eastward_stability,
    northward_stability,
    sun_height_ratio,
    extinction_coeff,
    reflectivity_ratio,
    insolation_source,
    daylight_tally,
    daylight_permutation,
):
    levels, rows, lanes = thermal_deviation.shape
    pad = 2
    lat_count, lon_count = lax.axis_size("lat"), lax.axis_size("lon")
    flat = lambda x: x.reshape(levels * rows, lanes)
    t, q, cx, cy = (
        flat(x)
        for x in (thermal_deviation, moisture_deviation, eastward_stability, northward_stability)
    )
    to_a, to_b, copies = edge_rows(
        rows,
        daylight_tally,
        daylight_permutation,
        t,
        q,
        cx,
        cy,
        sun_height_ratio,
        jnp.transpose(extinction_coeff),
        reflectivity_ratio.reshape(1, -1),
        insolation_source.reshape(1, -1),
    )
    lat_a = lax.ppermute(to_a, "lat", swaps(lat_count, 0, False))
    lat_b = lax.ppermute(to_b, ("lon", "lat"), odd_swaps(lat_count, lon_count))
    factor, *tables, scale, ft, fq, fx, fy, own = prepare(*copies, pad)
    groups = extinction_coeff.shape[0] // 16
    early = min(EARLY, groups - 1)
    sums = heating(*tables, 0, early)
    edges, to_a, to_b = edge_columns(ft, fq, own, lat_a, lat_b, sums, rows, pad)
    lon_b = lax.ppermute(to_b, "lon", swaps(lon_count, 1, True))
    lon_a = lax.ppermute(to_a, "lon", swaps(lon_count, 0, True))
    warming = heating(*tables, early, groups, (sums, factor, scale, edges))
    t_next, q_next = advect(ft, fq, fx, fy, edges, lat_a, lat_b, lon_a, lon_b, rows, pad)
    whole = lambda x: x.reshape(levels, rows, lanes)
    return whole(t_next), whole(q_next), whole(warming)


def solution(mesh):
    volume, surface = P(None, "lat", "lon"), P("lat", "lon")
    placed = (volume,) * 4 + (surface, P(), P(), P(), surface, P("lat", "lon", None))
    step = jax.shard_map(
        local, mesh=mesh, in_specs=placed, out_specs=(volume,) * 3, check_vma=False
    )
    return step
```

```python
import functools
import math

import jax
import jax.numpy as jnp
import ml_dtypes
import numpy as np
from jax import lax
from jax.experimental import pallas as pl
from jax.experimental.pallas import tpu as pltpu
from jax.sharding import PartitionSpec as P

heat_coeff = 20.0
f32, bf16 = jnp.float32, jnp.bfloat16
HELD = pltpu.VMEM
VMEM_SPEC = pl.BlockSpec(memory_space=pltpu.VMEM)
SMEM_SPEC = pl.BlockSpec(memory_space=pltpu.SMEM)
NT_DIMS = (((1,), (1,)), ((), ()))
TN_DIMS = (((0,), (0,)), ((), ()))


def iota(shape, dim):
    return lax.broadcasted_iota(jnp.int32, shape, dim)


def shape_of(*dims):
    return jax.ShapeDtypeStruct(dims, f32)


def held(*arrays):
    return [pltpu.with_memory_space_constraint(x, pltpu.VMEM) for x in arrays]


def swaps(count, first, ring):
    pairs = []
    for i in range(first, count, 2):
        j = i + 1
        if j == count and not ring:
            break
        pairs += [(i, j % count), (j % count, i)]
    return pairs


def odd_swaps(lat_count, lon_count):
    pairs = []
    for lon in range(lon_count):
        pairs += [(lon * lat_count + i, lon * lat_count + j) for i, j in swaps(lat_count, 1, False)]
        beside = lon + 1 if lon % 2 == 0 else lon - 1
        ends = {0} | ({lat_count - 1} if lat_count % 2 == 0 else set())
        pairs += [(lon * lat_count + end, beside * lat_count + end) for end in sorted(ends)]
    return pairs


def put_rows(blocks, rows, high_side, out):
    levels = blocks[0].shape[0] // rows
    t, q, cx, cy = blocks
    for k, (ref, deep) in enumerate(((t, 0), (t, 1), (q, 0), (q, 1), (cx, 0), (cy, 0))):
        high, low = (ref[pl.ds(r, levels, stride=rows), :] for r in (rows - 1 - deep, deep))
        out[k * levels : (k + 1) * levels, :] = jnp.where(high_side, high, low)


def rows_kernel(rows, tally, perm, *refs):
    count = (len(refs) - 3) // 2
    inputs, (to_a, to_b, sunlit), copies = refs[:count], refs[count : count + 3], refs[count + 3 :]
    even = lax.rem(lax.axis_index("lat"), 2) == 0
    put_rows(inputs[:4], rows, even, to_a)
    put_rows(inputs[:4], rows, jnp.logical_not(even), to_b)
    sunlit[...] = jnp.where(iota(perm.shape, 2) < tally[0, 0], perm[...], -1)
    for ref, copy in zip(inputs, copies):
        copy[...] = ref[...]


def edge_rows(rows, tally, perm, *arrays):
    total, lanes = arrays[0].shape
    sent = HELD((6 * (total // rows), lanes), f32)
    to_a, to_b, sunlit, *copies = pl.pallas_call(
        functools.partial(rows_kernel, rows),
        out_shape=(sent, sent, *(HELD(x.shape, x.dtype) for x in (perm, *arrays))),
        in_specs=[SMEM_SPEC] + [VMEM_SPEC] * (1 + len(arrays)),
        out_specs=(VMEM_SPEC,) * (3 + len(arrays)),
        name="edge_rows",
    )(tally, perm, *arrays)
    return to_a, to_b, (*copies, sunlit)


def halves(x):
    high = x.astype(bf16)
    return high, (x - high.astype(f32)).astype(bf16)


def thirds(value):
    left, parts = np.float32(value), []
    for _ in range(3):
        part = np.float32(left.astype(ml_dtypes.bfloat16))
        parts.append(float(part))
        left = np.float32(left - part)
    return parts


def pick_edges(slots, lanes, blocks):
    zero = jnp.zeros((1, blocks[0].shape[0]), f32)
    edges = [zero] * 16
    for block, at in zip(blocks, slots):
        by_lane = jnp.transpose(block)
        for deep, k in enumerate(at):
            edges[k] = by_lane[lanes - 1 - deep : lanes - deep]
            edges[8 + k] = by_lane[deep : deep + 1]
    return jnp.concatenate(edges, axis=0)


def prepare_kernel(
    pad, t, q, cx, cy, mu, k, albedo, solar, sunlit,
    factor, linear, tables, masks, shares, albedos, scale, ft, fq, fx, fy, own,
):
    levels, gpoints = k.shape
    rows, lanes = mu.shape
    tall = rows + 2 * pad
    blocks = (t, q, cx, cy)
    for ref, out in zip(blocks, (ft, fq, fx, fy)):
        for r in range(rows):
            out[pl.ds(pad + r, levels, stride=tall), :] = ref[pl.ds(r, levels, stride=rows), :]
    own[...] = pick_edges(((0, 1), (2, 3), (4,), (5,)), lanes, [ref[...] for ref in blocks])

    found = jnp.zeros((8, lanes), f32)
    for r in range(rows):
        column = sunlit[0, :, r * lanes : (r + 1) * lanes]
        row_at = jnp.where(column < 0, -1, column // lanes)
        lane_at = lax.rem(column, lanes)
        at_row = jnp.where(row_at == iota((8, lanes), 0), 1.0, 0.0).astype(bf16)
        at_lane = jnp.where(lane_at == iota((lanes, lanes), 0), 1.0, 0.0).astype(bf16)
        found += lax.dot_general(at_row, at_lane, NT_DIMS, preferred_element_type=f32)
    scale[...] = heat_coeff * mu[...] * found[:rows]

    quarter = lanes // 4
    factor[...] = (1.5 + jnp.tanh(q[...])) * (1.0 + 0.25 * jnp.tanh(t[...]))
    ones = jnp.ones((quarter, lanes), bf16)
    for r in range(rows):
        level_factor = factor[pl.ds(r, levels, stride=rows), :]
        per_path = level_factor * (-math.log2(math.e) / mu[r : r + 1, :])
        for start, value in ((0, level_factor), (lanes, per_path)):
            high, low = halves(value)
            linear[start : start + lanes, r * lanes : (r + 1) * lanes] = jnp.concatenate(
                [high, high, low, ones], axis=0
            )
    square = iota((gpoints, gpoints), 0) == iota((gpoints, gpoints), 1)

    def upright(row):
        return jnp.sum(jnp.where(square, row, 0.0), axis=1, keepdims=True)

    w = upright(albedo[...])
    filled = jnp.concatenate([k[...], jnp.zeros((levels, lanes - gpoints), f32)], axis=1)
    coeff = jnp.transpose(filled)[:gpoints]
    slot = iota((1, quarter), 1)

    def table(value, constants):
        high = value.astype(bf16).astype(f32)
        tail = jnp.zeros((1, quarter), f32)
        for i, c in enumerate(constants):
            tail = jnp.where(slot == i, c, tail)
        tail = jnp.broadcast_to(tail, (gpoints, quarter))
        return jnp.concatenate([high, value - high, high, tail], axis=1).astype(bf16)

    tables[0] = table(coeff, thirds(1.0 / 3.0))
    tables[1] = table(1.5 * (1.0 - w) * coeff, (0.75,))
    shares[...] = (1.0 - w) * upright(solar[...]) * coeff
    albedos[...] = jnp.broadcast_to(1.5 * w, (gpoints, lanes))
    lane = iota((16, lanes), 1)
    level, constant = lax.rem(lane, quarter), lane >= 3 * quarter
    for l in range(levels):
        masks[0, l] = jnp.where(constant | (level == l) | (level == l + 1), 1.0, 0.0).astype(bf16)
        masks[1, l] = jnp.where(constant | (level == l), 1.0, 0.0).astype(bf16)
        masks[2, l] = jnp.where(
            constant, 0.0, jnp.where(level < l, 1.0, jnp.where(level == l, 0.5, 0.0))
        ).astype(bf16)


def prepare(t, q, cx, cy, mu, k, albedo, solar, sunlit, pad):
    levels, gpoints = k.shape
    rows, lanes = mu.shape
    tall = levels * (rows + 2 * pad)
    return pl.pallas_call(
        functools.partial(prepare_kernel, pad),
        out_shape=(
            HELD(t.shape, f32),
            HELD((2 * lanes, rows * lanes), bf16),
            HELD((2, gpoints, lanes), bf16),
            HELD((3, levels, 16, lanes), bf16),
            HELD((gpoints, levels), f32),
            HELD((gpoints, lanes), f32),
            HELD((rows, lanes), f32),
            *[HELD((tall, lanes), f32)] * 4,
            HELD((16, levels * rows), f32),
        ),
        in_specs=[VMEM_SPEC] * 9,
        out_specs=(VMEM_SPEC,) * 12,
        cost_estimate=pl.CostEstimate(flops=1 << 22, bytes_accessed=1 << 21, transcendentals=1 << 17),
        name="prepare",
    )(*held(t, q, cx, cy, mu, k, albedo, solar, sunlit))


def by_side(even, first, last, from_a, from_b, k, levels, low, high):
    a, b = from_a[k * levels : (k + 1) * levels, :], from_b[k * levels : (k + 1) * levels, :]
    south, north = jnp.where(even, b, a), jnp.where(even, a, b)
    return jnp.where(first, low, south), jnp.where(last, high, north)


def lat_place():
    lat = lax.axis_index("lat")
    return lax.rem(lat, 2) == 0, lat == 0, lat == lax.axis_size("lat") - 1


def columns_kernel(pad, ft, fq, own, from_a, from_b, _, edges, to_a, to_b, ring):
    levels = from_a.shape[0] // 6
    total, lanes = ring.shape[1:]
    rows = total // levels
    tall = rows + 2 * pad
    ring[...] = jnp.zeros_like(ring)
    for i, ref in enumerate((ft, fq)):
        low, high = (ref[pl.ds(pad + r, levels, stride=tall), :] for r in (0, rows - 1))
        south, north = by_side(*lat_place(), from_a, from_b, 2 * i, levels, low, high)
        ring[i, pl.ds(0, levels, stride=rows), :] = south
        ring[i, pl.ds(rows - 1, levels, stride=rows), :] = north
    both = own[...] + pick_edges(((6,), (7,)), lanes, [ring[0], ring[1]])
    edges[...] = both
    even_lon = lax.rem(lax.axis_index("lon"), 2) == 0
    east, west = both[:8], both[8:]
    to_a[...] = jnp.where(even_lon, east, west)
    to_b[...] = jnp.where(even_lon, west, east)


def edge_columns(ft, fq, own, from_a, from_b, after, rows, pad):
    lanes = ft.shape[1]
    total = own.shape[1]
    return pl.pallas_call(
        functools.partial(columns_kernel, pad),
        out_shape=(HELD((16, total), f32), HELD((8, total), f32), HELD((8, total), f32)),
        in_specs=[VMEM_SPEC] * 6,
        out_specs=(VMEM_SPEC,) * 3,
        scratch_shapes=[pltpu.VMEM((2, total, lanes), f32)],
        name="edge_columns",
    )(*held(ft, fq, own, from_a, from_b, after))


def weights(cx, cy):
    hx, hy = 0.5 * cx, 0.5 * cy
    sx, sy = hx * cx, hy * cy
    return 1.0 - 2.0 * (sx + sy), sx - hx, sx + hx, sy - hy, sy + hy


def blend(w, here, east, west, north, south):
    return w[0] * here + w[1] * east + w[2] * west + w[3] * north + w[4] * south


def advect_kernel(
    rows, pad, ft, fq, fx, fy, edges, lat_a, lat_b, lon_a, lon_b, t_out, q_out, gt, gq, gx, gy, st, sq
):
    lanes = ft.shape[1]
    high = rows + 2 * pad
    levels = ft.shape[0] // high
    total = levels * rows
    place = lat_place()
    _, first, last = place
    grids = (gt, gq, gx, gy)
    for ref, grid, at in zip((ft, fq, fx, fy), grids, ((0, 1), (2, 3), (4,), (5,))):
        grid[...] = ref[...]
        low, top = (ref[pl.ds(pad + r, levels, stride=high), :] for r in (0, rows - 1))
        for deep in range(pad):
            k = at[min(deep, len(at) - 1)]
            south, north = by_side(*place, lat_a, lat_b, k, levels, low, top)
            grid[pl.ds(pad - 1 - deep, levels, stride=high), :] = south
            grid[pl.ds(pad + rows + deep, levels, stride=high), :] = north
    even_lon = lax.rem(lax.axis_index("lon"), 2) == 0
    a, b = lon_a[...], lon_b[...]
    east, west = jnp.where(even_lon, a, b), jnp.where(even_lon, b, a)
    mine = edges[...]

    def strip(x, k):
        return x[k : k + 1, :]

    row_of = lax.rem(iota((1, total), 1), rows)

    def up(x, k):
        return jnp.where(row_of == rows - 1, strip(x, 6 + k // 2), pltpu.roll(strip(x, k), total - 1, 1))

    def down(x, k):
        return jnp.where(row_of == 0, strip(x, 6 + k // 2), pltpu.roll(strip(x, k), 1, 1))

    ww = weights(strip(west, 4), strip(west, 5))
    we = weights(strip(east, 4), strip(east, 5))
    firsts = []
    for k in (0, 2):
        firsts.append(blend(ww, strip(west, k), strip(mine, 8 + k), strip(west, k + 1), up(west, k), down(west, k)))
        firsts.append(blend(we, strip(east, k), strip(east, k + 1), strip(mine, k), up(east, k), down(east, k)))
    columns = [strip(x, k) for k in (0, 2, 6, 7) for x in (east, west)]
    columns += [firsts[i] for i in (1, 0, 3, 2)]
    stack = jnp.concatenate(columns + [jnp.zeros((lanes - len(columns), total), f32)], axis=0)
    by_lane = jnp.transpose(stack)
    spread = (st, sq)
    cut = lambda x: x.reshape(levels, high, lanes)
    flat = lambda i: pltpu.roll(by_lane, lanes - 1 - 2 * i, 1)
    w = weights(cut(gx[...]), cut(gy[...]))
    full = (levels, high, lanes)
    lane, at = iota(full, 2), iota(full, 1)
    for k, (ref, out, rim_ref) in enumerate(((gt, t_out, st), (gq, q_out, sq))):
        f = cut(ref[...])
        for step in range(2):
            rim_ref[step, 0] = flat((0, 4)[step] + k)
            if step == 0:
                rim_ref[step, 1] = flat(2 + k)
            tall_rim = ref
            for r in range(rows):
                tall_rim[pl.ds(pad + r, levels, stride=high), :] = rim_ref[step, 0, pl.ds(r, levels, stride=rows), :]
            if step == 0:
                tall_rim[pl.ds(pad - 1, levels, stride=high), :] = rim_ref[step, 1, pl.ds(0, levels, stride=rows), :]
                tall_rim[pl.ds(pad + rows, levels, stride=high), :] = rim_ref[
                    step, 1, pl.ds(rows - 1, levels, stride=rows), :
                ]
            rim = cut(tall_rim[...])
            e = jnp.where(lane == lanes - 1, rim, pltpu.roll(f, lanes - 1, 2))
            wst = jnp.where(lane == 0, rim, pltpu.roll(f, 1, 2))
            n = jnp.where(last & (at == pad + rows - 1), f, pltpu.roll(f, high - 1, 1))
            s = jnp.where(first & (at == pad), f, pltpu.roll(f, 1, 1))
            f = blend(w, f, e, wst, n, s)
        ref[...] = f.reshape(levels * high, lanes)
        for r in range(rows):
            out[pl.ds(r, levels, stride=rows), :] = ref[pl.ds(pad + r, levels, stride=high), :]


def advect(ft, fq, fx, fy, edges, lat_a, lat_b, lon_a, lon_b, rows, pad):
    tall, lanes = ft.shape
    total = edges.shape[1]
    grid = pltpu.VMEM((tall, lanes), f32)
    return pl.pallas_call(
        functools.partial(advect_kernel, rows, pad),
        out_shape=(shape_of(total, lanes), shape_of(total, lanes)),
        in_specs=[VMEM_SPEC] * 9,
        out_specs=(VMEM_SPEC,) * 2,
        scratch_shapes=[grid] * 4 + [pltpu.VMEM((2, 2, total, lanes), f32)] * 2,
        name="advect",
    )(*held(ft, fq, fx, fy, edges, lat_a, lat_b, lon_a, lon_b))

SLOTS, AHEAD = 16, 8
EARLY = 5


def heating_kernel(
    begin, end, linear, tables, masks, shares, albedos, *refs
):
    gpoints, levels = shares.shape
    lanes = albedos.shape[1]
    rows = linear.shape[1] // lanes
    if begin == 0:
        total, trans, pull, beam = refs
    else:
        so_far, factor, scale, _, out, trans, pull, beam, total = refs
    wide = 2 * lanes
    engines = rows // 2
    total[...] = jnp.zeros_like(total) if begin == 0 else so_far[...]
    units = [(a, b) for a in range(2) for b in range(rows)]
    each = range(len(units))

    def main(*sums):
        def at(m, l):
            return sums[m * SLOTS + l % SLOTS]

        blank = jnp.zeros((16, lanes), bf16)

        def issue(i, l):
            start = pl.multiple_of(i * 16, 16)
            plain, absorbing = (tables[j, pl.ds(start, 16), :] for j in range(2))
            stack = [
                jnp.concatenate([plain * masks[0, l], blank], axis=1),
                jnp.concatenate([absorbing * masks[1, l], blank], axis=1),
                jnp.concatenate([blank, plain * masks[2, l]], axis=1),
            ]
            stack = jnp.concatenate(stack, axis=0)
            for m in range(engines):
                pltpu.matmul_acc_lhs(at(m, l), stack)

        def group(i):
            start = pl.multiple_of(i * 16, 16)
            starts = [pl.multiple_of(start + 8 * a, 8) for a in range(2)]
            w15 = [albedos[pl.ds(s, 8), :] for s in starts]
            share = [shares[pl.ds(s, 8), :] for s in starts]
            following = jnp.minimum(i + 1, end - 1)
            y = current = step = None
            for l in range(levels):
                if l + AHEAD < levels:
                    issue(i, l + AHEAD)
                popped = [pltpu.matmul_pop(at(m, l)) for m in range(engines)]

                def part(kind, a, b):
                    s = kind * 16 + a * 8
                    return popped[b // 2][s : s + 8, (b % 2) * lanes : (b % 2 + 1) * lanes]

                resist, shunt, path = ([part(i, a, b) for a, b in units] for i in range(3))
                direct = [jnp.exp2(p) for p in path]
                source = [w15[units[u][0]] * direct[u] for u in each]
                for u in each:
                    beam[u, l] = direct[u]
                if l == 0:
                    y, current = shunt, source
                else:
                    y = [shunt[u] + y[u] * step[u] for u in each]
                    current = [source[u] + current[u] * step[u] for u in each]
                if l < levels - 1:
                    step = [1.0 / (1.0 + resist[u] * y[u]) for u in each]
                    for u in each:
                        trans[u, l] = step[u]
                        pull[u, l] = resist[u] * current[u]
            diffuse = [current[u] / y[u] for u in each]
            for l in range(levels - 1, -1, -1):
                if levels - 1 - l < AHEAD:
                    issue(following, levels - 1 - l)
                if l < levels - 1:
                    diffuse = [trans[u, l] * (pull[u, l] + diffuse[u]) for u in each]
                spread = [jnp.broadcast_to(share[a][:, l : l + 1], (8, lanes)) for a in range(2)]
                for b in range(rows):
                    pair = [
                        (diffuse[a * rows + b] + beam[a * rows + b, l]) * spread[a]
                        for a in range(2)
                    ]
                    total[l, b] = total[l, b] + (pair[0] + pair[1])

        nothing = jnp.zeros((16, wide), bf16)
        for m in range(engines):
            last = sums[engines * SLOTS + m]
            pltpu.matmul_push_rhs(linear[:, m * wide : (m + 1) * wide], 0, m)
            pltpu.matmul_acc_lhs(last, nothing, load_staged_rhs=0)
            pltpu.matmul_pop(last)
        for l in range(AHEAD):
            issue(begin, l)
        pl.loop(begin, end)(group)
        for l in range(AHEAD):
            for m in range(engines):
                pltpu.matmul_pop(at(m, l))

    pl.run_scoped(
        main,
        *[pltpu.ACC(m)((48, wide), f32) for m in range(engines) for _ in range(SLOTS)],
        *[pltpu.ACC(m)((16, wide), f32) for m in range(engines)],
    )
    if begin == 0:
        return
    column_scale = scale[...]
    for l in range(levels):
        here = pl.ds(l * rows, rows)
        out[here, :] = jnp.sum(total[l], axis=1) * column_scale * factor[here, :]


def heating(linear, tables, masks, shares, albedos, begin, end, more=()):
    gpoints, levels = shares.shape
    lanes = albedos.shape[1]
    rows = linear.shape[1] // lanes
    stage = pltpu.VMEM((2 * rows, levels, 8, lanes), f32)
    sums = (levels, rows, 8, lanes)
    cells = (end - begin) * 16 * levels * rows * lanes
    return pl.pallas_call(
        functools.partial(heating_kernel, begin, end),
        out_shape=shape_of(levels * rows, lanes) if more else HELD(sums, f32),
        in_specs=[VMEM_SPEC] * (5 + len(more)),
        out_specs=VMEM_SPEC,
        scratch_shapes=[stage, stage, stage] + [pltpu.VMEM(sums, f32)] * bool(more),
        cost_estimate=pl.CostEstimate(flops=640 * cells, bytes_accessed=1 << 20, transcendentals=2 * cells),
        name="heating",
    )(*held(linear, tables, masks, shares, albedos, *more))


def local(
    thermal_deviation,
    moisture_deviation,
    eastward_stability,
    northward_stability,
    sun_height_ratio,
    extinction_coeff,
    reflectivity_ratio,
    insolation_source,
    daylight_tally,
    daylight_permutation,
):
    levels, rows, lanes = thermal_deviation.shape
    pad = 2
    lat_count, lon_count = lax.axis_size("lat"), lax.axis_size("lon")
    flat = lambda x: x.reshape(levels * rows, lanes)
    t, q, cx, cy = (
        flat(x)
        for x in (thermal_deviation, moisture_deviation, eastward_stability, northward_stability)
    )
    to_a, to_b, copies = edge_rows(
        rows,
        daylight_tally,
        daylight_permutation,
        t,
        q,
        cx,
        cy,
        sun_height_ratio,
        jnp.transpose(extinction_coeff),
        reflectivity_ratio.reshape(1, -1),
        insolation_source.reshape(1, -1),
    )
    lat_a = lax.ppermute(to_a, "lat", swaps(lat_count, 0, False))
    lat_b = lax.ppermute(to_b, ("lon", "lat"), odd_swaps(lat_count, lon_count))
    factor, *tables, scale, ft, fq, fx, fy, own = prepare(*copies, pad)
    groups = extinction_coeff.shape[0] // 16
    early = min(EARLY, groups - 1)
    sums = heating(*tables, 0, early)
    edges, to_a, to_b = edge_columns(ft, fq, own, lat_a, lat_b, sums, rows, pad)
    lon_b = lax.ppermute(to_b, "lon", swaps(lon_count, 1, True))
    lon_a = lax.ppermute(to_a, "lon", swaps(lon_count, 0, True))
    warming = heating(*tables, early, groups, (sums, factor, scale, edges))
    t_next, q_next = advect(ft, fq, fx, fy, edges, lat_a, lat_b, lon_a, lon_b, rows, pad)
    whole = lambda x: x.reshape(levels, rows, lanes)
    return whole(t_next), whole(q_next), whole(warming)


def solution(mesh):
    volume, surface = P(None, "lat", "lon"), P("lat", "lon")
    placed = (volume,) * 4 + (surface, P(), P(), P(), surface, P("lat", "lon", None))
    step = jax.shard_map(
        local, mesh=mesh, in_specs=placed, out_specs=(volume,) * 3, check_vma=False
    )
    return step
```

```python
import functools
import math

import jax
import jax.numpy as jnp
import ml_dtypes
import numpy as np
from jax import lax
from jax.experimental import pallas as pl
from jax.experimental.pallas import tpu as pltpu
from jax.sharding import PartitionSpec as P

heat_coeff = 20.0
f32, bf16 = jnp.float32, jnp.bfloat16
HELD = pltpu.VMEM
VMEM_SPEC = pl.BlockSpec(memory_space=pltpu.VMEM)
SMEM_SPEC = pl.BlockSpec(memory_space=pltpu.SMEM)
NT_DIMS = (((1,), (1,)), ((), ()))
TN_DIMS = (((0,), (0,)), ((), ()))


def iota(shape, dim):
    return lax.broadcasted_iota(jnp.int32, shape, dim)


def shape_of(*dims):
    return jax.ShapeDtypeStruct(dims, f32)


def held(*arrays):
    return [pltpu.with_memory_space_constraint(x, pltpu.VMEM) for x in arrays]


def swaps(count, first, ring):
    pairs = []
    for i in range(first, count, 2):
        j = i + 1
        if j == count and not ring:
            break
        pairs += [(i, j % count), (j % count, i)]
    return pairs


def odd_swaps(lat_count, lon_count):
    pairs = []
    for lon in range(lon_count):
        pairs += [(lon * lat_count + i, lon * lat_count + j) for i, j in swaps(lat_count, 1, False)]
        beside = lon + 1 if lon % 2 == 0 else lon - 1
        ends = {0} | ({lat_count - 1} if lat_count % 2 == 0 else set())
        pairs += [(lon * lat_count + end, beside * lat_count + end) for end in sorted(ends)]
    return pairs


def put_rows(blocks, rows, high_side, out):
    levels = blocks[0].shape[0] // rows
    t, q, cx, cy = blocks
    for k, (ref, deep) in enumerate(((t, 0), (t, 1), (q, 0), (q, 1), (cx, 0), (cy, 0))):
        high, low = (ref[pl.ds(r, levels, stride=rows), :] for r in (rows - 1 - deep, deep))
        out[k * levels : (k + 1) * levels, :] = jnp.where(high_side, high, low)


def rows_kernel(rows, tally, perm, *refs):
    count = (len(refs) - 3) // 2
    inputs, (to_a, to_b, sunlit), copies = refs[:count], refs[count : count + 3], refs[count + 3 :]
    even = lax.rem(lax.axis_index("lat"), 2) == 0
    put_rows(inputs[:4], rows, even, to_a)
    put_rows(inputs[:4], rows, jnp.logical_not(even), to_b)
    sunlit[...] = jnp.where(iota(perm.shape, 2) < tally[0, 0], perm[...], -1)
    for ref, copy in zip(inputs, copies):
        copy[...] = ref[...]


def edge_rows(rows, tally, perm, *arrays):
    total, lanes = arrays[0].shape
    sent = HELD((6 * (total // rows), lanes), f32)
    to_a, to_b, sunlit, *copies = pl.pallas_call(
        functools.partial(rows_kernel, rows),
        out_shape=(sent, sent, *(HELD(x.shape, x.dtype) for x in (perm, *arrays))),
        in_specs=[SMEM_SPEC] + [VMEM_SPEC] * (1 + len(arrays)),
        out_specs=(VMEM_SPEC,) * (3 + len(arrays)),
        name="edge_rows",
    )(tally, perm, *arrays)
    return to_a, to_b, (*copies, sunlit)


def halves(x):
    high = x.astype(bf16)
    return high, (x - high.astype(f32)).astype(bf16)


def thirds(value):
    left, parts = np.float32(value), []
    for _ in range(3):
        part = np.float32(left.astype(ml_dtypes.bfloat16))
        parts.append(float(part))
        left = np.float32(left - part)
    return parts


def pick_edges(slots, lanes, blocks):
    zero = jnp.zeros((1, blocks[0].shape[0]), f32)
    edges = [zero] * 16
    for block, at in zip(blocks, slots):
        by_lane = jnp.transpose(block)
        for deep, k in enumerate(at):
            edges[k] = by_lane[lanes - 1 - deep : lanes - deep]
            edges[8 + k] = by_lane[deep : deep + 1]
    return jnp.concatenate(edges, axis=0)


def prepare_kernel(
    pad, t, q, cx, cy, mu, k, albedo, solar, sunlit,
    factor, linear, tables, masks, shares, albedos, scale, ft, fq, fx, fy, own,
):
    levels, gpoints = k.shape
    rows, lanes = mu.shape
    tall = rows + 2 * pad
    blocks = (t, q, cx, cy)
    for ref, out in zip(blocks, (ft, fq, fx, fy)):
        for r in range(rows):
            out[pl.ds(pad + r, levels, stride=tall), :] = ref[pl.ds(r, levels, stride=rows), :]
    own[...] = pick_edges(((0, 1), (2, 3), (4,), (5,)), lanes, [ref[...] for ref in blocks])

    found = jnp.zeros((8, lanes), f32)
    for r in range(rows):
        column = sunlit[0, :, r * lanes : (r + 1) * lanes]
        row_at = jnp.where(column < 0, -1, column // lanes)
        lane_at = lax.rem(column, lanes)
        at_row = jnp.where(row_at == iota((8, lanes), 0), 1.0, 0.0).astype(bf16)
        at_lane = jnp.where(lane_at == iota((lanes, lanes), 0), 1.0, 0.0).astype(bf16)
        found += lax.dot_general(at_row, at_lane, NT_DIMS, preferred_element_type=f32)
    scale[...] = heat_coeff * mu[...] * found[:rows]

    quarter = lanes // 4
    factor[...] = (1.5 + jnp.tanh(q[...])) * (1.0 + 0.25 * jnp.tanh(t[...]))
    ones = jnp.ones((quarter, lanes), bf16)
    for r in range(rows):
        level_factor = factor[pl.ds(r, levels, stride=rows), :]
        per_path = level_factor * (-math.log2(math.e) / mu[r : r + 1, :])
        for start, value in ((0, level_factor), (lanes, per_path)):
            high, low = halves(value)
            linear[start : start + lanes, r * lanes : (r + 1) * lanes] = jnp.concatenate(
                [high, high, low, ones], axis=0
            )
    square = iota((gpoints, gpoints), 0) == iota((gpoints, gpoints), 1)

    def upright(row):
        return jnp.sum(jnp.where(square, row, 0.0), axis=1, keepdims=True)

    w = upright(albedo[...])
    filled = jnp.concatenate([k[...], jnp.zeros((levels, lanes - gpoints), f32)], axis=1)
    coeff = jnp.transpose(filled)[:gpoints]
    slot = iota((1, quarter), 1)

    def table(value, constants):
        high = value.astype(bf16).astype(f32)
        tail = jnp.zeros((1, quarter), f32)
        for i, c in enumerate(constants):
            tail = jnp.where(slot == i, c, tail)
        tail = jnp.broadcast_to(tail, (gpoints, quarter))
        return jnp.concatenate([high, value - high, high, tail], axis=1).astype(bf16)

    tables[0] = table(coeff, thirds(1.0 / 3.0))
    tables[1] = table(1.5 * (1.0 - w) * coeff, (0.75,))
    shares[...] = (1.0 - w) * upright(solar[...]) * coeff
    albedos[...] = jnp.broadcast_to(1.5 * w, (gpoints, lanes))
    lane = iota((16, lanes), 1)
    level, constant = lax.rem(lane, quarter), lane >= 3 * quarter
    for l in range(levels):
        masks[0, l] = jnp.where(constant | (level == l) | (level == l + 1), 1.0, 0.0).astype(bf16)
        masks[1, l] = jnp.where(constant | (level == l), 1.0, 0.0).astype(bf16)
        masks[2, l] = jnp.where(
            constant, 0.0, jnp.where(level < l, 1.0, jnp.where(level == l, 0.5, 0.0))
        ).astype(bf16)


def prepare(t, q, cx, cy, mu, k, albedo, solar, sunlit, pad):
    levels, gpoints = k.shape
    rows, lanes = mu.shape
    tall = levels * (rows + 2 * pad)
    return pl.pallas_call(
        functools.partial(prepare_kernel, pad),
        out_shape=(
            HELD(t.shape, f32),
            HELD((2 * lanes, rows * lanes), bf16),
            HELD((2, gpoints, lanes), bf16),
            HELD((3, levels, 16, lanes), bf16),
            HELD((gpoints, levels), f32),
            HELD((gpoints, lanes), f32),
            HELD((rows, lanes), f32),
            *[HELD((tall, lanes), f32)] * 4,
            HELD((16, levels * rows), f32),
        ),
        in_specs=[VMEM_SPEC] * 9,
        out_specs=(VMEM_SPEC,) * 12,
        cost_estimate=pl.CostEstimate(flops=1 << 22, bytes_accessed=1 << 21, transcendentals=1 << 17),
        name="prepare",
    )(*held(t, q, cx, cy, mu, k, albedo, solar, sunlit))


def by_side(even, first, last, from_a, from_b, k, levels, low, high):
    a, b = from_a[k * levels : (k + 1) * levels, :], from_b[k * levels : (k + 1) * levels, :]
    south, north = jnp.where(even, b, a), jnp.where(even, a, b)
    return jnp.where(first, low, south), jnp.where(last, high, north)


def lat_place():
    lat = lax.axis_index("lat")
    return lax.rem(lat, 2) == 0, lat == 0, lat == lax.axis_size("lat") - 1


def columns_kernel(pad, ft, fq, own, from_a, from_b, _, edges, to_a, to_b, ring):
    levels = from_a.shape[0] // 6
    total, lanes = ring.shape[1:]
    rows = total // levels
    tall = rows + 2 * pad
    ring[...] = jnp.zeros_like(ring)
    for i, ref in enumerate((ft, fq)):
        low, high = (ref[pl.ds(pad + r, levels, stride=tall), :] for r in (0, rows - 1))
        south, north = by_side(*lat_place(), from_a, from_b, 2 * i, levels, low, high)
        ring[i, pl.ds(0, levels, stride=rows), :] = south
        ring[i, pl.ds(rows - 1, levels, stride=rows), :] = north
    both = own[...] + pick_edges(((6,), (7,)), lanes, [ring[0], ring[1]])
    edges[...] = both
    even_lon = lax.rem(lax.axis_index("lon"), 2) == 0
    east, west = both[:8], both[8:]
    to_a[...] = jnp.where(even_lon, east, west)
    to_b[...] = jnp.where(even_lon, west, east)


def edge_columns(ft, fq, own, from_a, from_b, after, rows, pad):
    lanes = ft.shape[1]
    total = own.shape[1]
    return pl.pallas_call(
        functools.partial(columns_kernel, pad),
        out_shape=(HELD((16, total), f32), HELD((8, total), f32), HELD((8, total), f32)),
        in_specs=[VMEM_SPEC] * 6,
        out_specs=(VMEM_SPEC,) * 3,
        scratch_shapes=[pltpu.VMEM((2, total, lanes), f32)],
        name="edge_columns",
    )(*held(ft, fq, own, from_a, from_b, after))


def weights(cx, cy):
    hx, hy = 0.5 * cx, 0.5 * cy
    sx, sy = hx * cx, hy * cy
    return 1.0 - 2.0 * (sx + sy), sx - hx, sx + hx, sy - hy, sy + hy


def blend(w, here, east, west, north, south):
    return w[0] * here + w[1] * east + w[2] * west + w[3] * north + w[4] * south


def advect_kernel(
    rows, pad, ft, fq, fx, fy, edges, lat_a, lat_b, lon_a, lon_b, t_out, q_out, gt, gq, gx, gy, st, sq
):
    lanes = ft.shape[1]
    high = rows + 2 * pad
    levels = ft.shape[0] // high
    total = levels * rows
    place = lat_place()
    _, first, last = place
    grids = (gt, gq, gx, gy)
    for ref, grid, at in zip((ft, fq, fx, fy), grids, ((0, 1), (2, 3), (4,), (5,))):
        grid[...] = ref[...]
        low, top = (ref[pl.ds(pad + r, levels, stride=high), :] for r in (0, rows - 1))
        for deep in range(pad):
            k = at[min(deep, len(at) - 1)]
            south, north = by_side(*place, lat_a, lat_b, k, levels, low, top)
            grid[pl.ds(pad - 1 - deep, levels, stride=high), :] = south
            grid[pl.ds(pad + rows + deep, levels, stride=high), :] = north
    even_lon = lax.rem(lax.axis_index("lon"), 2) == 0
    a, b = lon_a[...], lon_b[...]
    east, west = jnp.where(even_lon, a, b), jnp.where(even_lon, b, a)
    mine = edges[...]

    def strip(x, k):
        return x[k : k + 1, :]

    row_of = lax.rem(iota((1, total), 1), rows)

    def up(x, k):
        return jnp.where(row_of == rows - 1, strip(x, 6 + k // 2), pltpu.roll(strip(x, k), total - 1, 1))

    def down(x, k):
        return jnp.where(row_of == 0, strip(x, 6 + k // 2), pltpu.roll(strip(x, k), 1, 1))

    ww = weights(strip(west, 4), strip(west, 5))
    we = weights(strip(east, 4), strip(east, 5))
    firsts = []
    for k in (0, 2):
        firsts.append(blend(ww, strip(west, k), strip(mine, 8 + k), strip(west, k + 1), up(west, k), down(west, k)))
        firsts.append(blend(we, strip(east, k), strip(east, k + 1), strip(mine, k), up(east, k), down(east, k)))
    columns = [strip(x, k) for k in (0, 2, 6, 7) for x in (east, west)]
    columns += [firsts[i] for i in (1, 0, 3, 2)]
    stack = jnp.concatenate(columns + [jnp.zeros((lanes - len(columns), total), f32)], axis=0)
    by_lane = jnp.transpose(stack)
    spread = (st, sq)
    cut = lambda x: x.reshape(levels, high, lanes)
    flat = lambda i: pltpu.roll(by_lane, lanes - 1 - 2 * i, 1)
    w = weights(cut(gx[...]), cut(gy[...]))
    full = (levels, high, lanes)
    lane, at = iota(full, 2), iota(full, 1)
    for k, (ref, out, rim_ref) in enumerate(((gt, t_out, st), (gq, q_out, sq))):
        f = cut(ref[...])
        for step in range(2):
            rim_ref[step, 0] = flat((0, 4)[step] + k)
            if step == 0:
                rim_ref[step, 1] = flat(2 + k)
            tall_rim = ref
            for r in range(rows):
                tall_rim[pl.ds(pad + r, levels, stride=high), :] = rim_ref[step, 0, pl.ds(r, levels, stride=rows), :]
            if step == 0:
                tall_rim[pl.ds(pad - 1, levels, stride=high), :] = rim_ref[step, 1, pl.ds(0, levels, stride=rows), :]
                tall_rim[pl.ds(pad + rows, levels, stride=high), :] = rim_ref[
                    step, 1, pl.ds(rows - 1, levels, stride=rows), :
                ]
            rim = cut(tall_rim[...])
            e = jnp.where(lane == lanes - 1, rim, pltpu.roll(f, lanes - 1, 2))
            wst = jnp.where(lane == 0, rim, pltpu.roll(f, 1, 2))
            n = jnp.where(last & (at == pad + rows - 1), f, pltpu.roll(f, high - 1, 1))
            s = jnp.where(first & (at == pad), f, pltpu.roll(f, 1, 1))
            f = blend(w, f, e, wst, n, s)
        ref[...] = f.reshape(levels * high, lanes)
        for r in range(rows):
            out[pl.ds(r, levels, stride=rows), :] = ref[pl.ds(pad + r, levels, stride=high), :]


def advect(ft, fq, fx, fy, edges, lat_a, lat_b, lon_a, lon_b, rows, pad):
    tall, lanes = ft.shape
    total = edges.shape[1]
    grid = pltpu.VMEM((tall, lanes), f32)
    return pl.pallas_call(
        functools.partial(advect_kernel, rows, pad),
        out_shape=(shape_of(total, lanes), shape_of(total, lanes)),
        in_specs=[VMEM_SPEC] * 9,
        out_specs=(VMEM_SPEC,) * 2,
        scratch_shapes=[grid] * 4 + [pltpu.VMEM((2, 2, total, lanes), f32)] * 2,
        name="advect",
    )(*held(ft, fq, fx, fy, edges, lat_a, lat_b, lon_a, lon_b))

SLOTS, AHEAD = 16, 8
EARLY = 5


def row_sums(tiles):
    row = iota(tiles[0].shape, 0)
    for far in (4, 2, 1):
        low = (row & far) == 0
        merged = []
        for a, b in zip(tiles[:far], tiles[far:]):
            other = jnp.where(low, b, a)
            back = pltpu.roll(other, far, 0)
            if far != 4:
                back = jnp.where(low, pltpu.roll(other, 8 - far, 0), back)
            merged.append(jnp.where(low, a, b) + back)
        tiles = merged
    return tiles[0]


def heating_kernel(
    begin, end, linear, tables, masks, shares, albedos, *refs
):
    gpoints, levels = shares.shape
    lanes = albedos.shape[1]
    rows = linear.shape[1] // lanes
    if begin == 0:
        total, trans, pull, beam = refs
    else:
        so_far, factor, scale, _, out, trans, pull, beam, total = refs
    wide = 2 * lanes
    engines = rows // 2
    total[...] = jnp.zeros_like(total) if begin == 0 else so_far[...]
    units = [(a, b) for a in range(2) for b in range(rows)]
    each = range(len(units))

    def main(*sums):
        def at(m, l):
            return sums[m * SLOTS + l % SLOTS]

        blank = jnp.zeros((16, lanes), bf16)

        def issue(i, l):
            start = pl.multiple_of(i * 16, 16)
            plain, absorbing = (tables[j, pl.ds(start, 16), :] for j in range(2))
            stack = [
                jnp.concatenate([plain * masks[0, l], blank], axis=1),
                jnp.concatenate([absorbing * masks[1, l], blank], axis=1),
                jnp.concatenate([blank, plain * masks[2, l]], axis=1),
            ]
            stack = jnp.concatenate(stack, axis=0)
            for m in range(engines):
                pltpu.matmul_acc_lhs(at(m, l), stack)

        def group(i, more=True):
            start = pl.multiple_of(i * 16, 16)
            starts = [pl.multiple_of(start + 8 * a, 8) for a in range(2)]
            w15 = [albedos[pl.ds(s, 8), :] for s in starts]
            share = [shares[pl.ds(s, 8), :] for s in starts]
            y = current = step = None
            for l in range(levels):
                if l + AHEAD < levels:
                    issue(i, l + AHEAD)
                popped = [pltpu.matmul_pop(at(m, l)) for m in range(engines)]

                def part(kind, a, b):
                    s = kind * 16 + a * 8
                    return popped[b // 2][s : s + 8, (b % 2) * lanes : (b % 2 + 1) * lanes]

                resist, shunt, path = ([part(i, a, b) for a, b in units] for i in range(3))
                direct = [jnp.exp2(p) for p in path]
                source = [w15[units[u][0]] * direct[u] for u in each]
                for u in each:
                    beam[u, l] = direct[u]
                if l == 0:
                    y, current = shunt, source
                else:
                    y = [shunt[u] + y[u] * step[u] for u in each]
                    current = [source[u] + current[u] * step[u] for u in each]
                if l < levels - 1:
                    step = [1.0 / (1.0 + resist[u] * y[u]) for u in each]
                    for u in each:
                        trans[u, l] = step[u]
                        pull[u, l] = resist[u] * current[u]
            diffuse = [current[u] / y[u] for u in each]
            for l in range(levels - 1, -1, -1):
                if more and levels - 1 - l < AHEAD:
                    issue(i + 1, levels - 1 - l)
                if l < levels - 1:
                    diffuse = [trans[u, l] * (pull[u, l] + diffuse[u]) for u in each]
                spread = [jnp.broadcast_to(share[a][:, l : l + 1], (8, lanes)) for a in range(2)]
                for b in range(rows):
                    pair = [
                        (diffuse[a * rows + b] + beam[a * rows + b, l]) * spread[a]
                        for a in range(2)
                    ]
                    total[l, b] = total[l, b] + (pair[0] + pair[1])

        nothing = jnp.zeros((16, wide), bf16)
        for m in range(engines):
            last = sums[engines * SLOTS + m]
            pltpu.matmul_push_rhs(linear[:, m * wide : (m + 1) * wide], 0, m)
            pltpu.matmul_acc_lhs(last, nothing, load_staged_rhs=0)
            pltpu.matmul_pop(last)
        for l in range(AHEAD):
            issue(begin, l)
        pl.loop(begin, end - 1)(group)
        group(end - 1, more=False)

    pl.run_scoped(
        main,
        *[pltpu.ACC(m)((48, wide), f32) for m in range(engines) for _ in range(SLOTS)],
        *[pltpu.ACC(m)((16, wide), f32) for m in range(engines)],
    )
    if begin == 0:
        return
    block = 8 // rows
    column_scale = jnp.concatenate([scale[...]] * block, axis=0)
    for l in range(0, levels, block):
        here = pl.ds(l * rows, 8)
        sums = row_sums([total[l + i, r] for i in range(block) for r in range(rows)])
        out[here, :] = sums * column_scale * factor[here, :]


def heating(linear, tables, masks, shares, albedos, begin, end, more=()):
    gpoints, levels = shares.shape
    lanes = albedos.shape[1]
    rows = linear.shape[1] // lanes
    stage = pltpu.VMEM((2 * rows, levels, 8, lanes), f32)
    sums = (levels, rows, 8, lanes)
    cells = (end - begin) * 16 * levels * rows * lanes
    return pl.pallas_call(
        functools.partial(heating_kernel, begin, end),
        out_shape=shape_of(levels * rows, lanes) if more else HELD(sums, f32),
        in_specs=[VMEM_SPEC] * (5 + len(more)),
        out_specs=VMEM_SPEC,
        scratch_shapes=[stage, stage, stage] + [pltpu.VMEM(sums, f32)] * bool(more),
        cost_estimate=pl.CostEstimate(flops=640 * cells, bytes_accessed=1 << 20, transcendentals=2 * cells),
        name="heating",
    )(*held(linear, tables, masks, shares, albedos, *more))


def local(
    thermal_deviation,
    moisture_deviation,
    eastward_stability,
    northward_stability,
    sun_height_ratio,
    extinction_coeff,
    reflectivity_ratio,
    insolation_source,
    daylight_tally,
    daylight_permutation,
):
    levels, rows, lanes = thermal_deviation.shape
    pad = 2
    lat_count, lon_count = lax.axis_size("lat"), lax.axis_size("lon")
    flat = lambda x: x.reshape(levels * rows, lanes)
    t, q, cx, cy = (
        flat(x)
        for x in (thermal_deviation, moisture_deviation, eastward_stability, northward_stability)
    )
    to_a, to_b, copies = edge_rows(
        rows,
        daylight_tally,
        daylight_permutation,
        t,
        q,
        cx,
        cy,
        sun_height_ratio,
        jnp.transpose(extinction_coeff),
        reflectivity_ratio.reshape(1, -1),
        insolation_source.reshape(1, -1),
    )
    lat_a = lax.ppermute(to_a, "lat", swaps(lat_count, 0, False))
    lat_b = lax.ppermute(to_b, ("lon", "lat"), odd_swaps(lat_count, lon_count))
    factor, *tables, scale, ft, fq, fx, fy, own = prepare(*copies, pad)
    groups = extinction_coeff.shape[0] // 16
    early = min(EARLY, groups - 1)
    sums = heating(*tables, 0, early)
    edges, to_a, to_b = edge_columns(ft, fq, own, lat_a, lat_b, sums, rows, pad)
    lon_b = lax.ppermute(to_b, "lon", swaps(lon_count, 1, True))
    lon_a = lax.ppermute(to_a, "lon", swaps(lon_count, 0, True))
    warming = heating(*tables, early, groups, (sums, factor, scale, edges))
    t_next, q_next = advect(ft, fq, fx, fy, edges, lat_a, lat_b, lon_a, lon_b, rows, pad)
    whole = lambda x: x.reshape(levels, rows, lanes)
    return whole(t_next), whole(q_next), whole(warming)


def solution(mesh):
    volume, surface = P(None, "lat", "lon"), P("lat", "lon")
    placed = (volume,) * 4 + (surface, P(), P(), P(), surface, P("lat", "lon", None))
    step = jax.shard_map(
        local, mesh=mesh, in_specs=placed, out_specs=(volume,) * 3, check_vma=False
    )
    return step
```

```python
import functools
import math

import jax
import jax.numpy as jnp
import ml_dtypes
import numpy as np
from jax import lax
from jax.experimental import pallas as pl
from jax.experimental.pallas import tpu as pltpu
from jax.sharding import PartitionSpec as P

heat_coeff = 20.0
f32, bf16 = jnp.float32, jnp.bfloat16
HELD = pltpu.VMEM
VMEM_SPEC = pl.BlockSpec(memory_space=pltpu.VMEM)
SMEM_SPEC = pl.BlockSpec(memory_space=pltpu.SMEM)
NT_DIMS = (((1,), (1,)), ((), ()))
TN_DIMS = (((0,), (0,)), ((), ()))


def iota(shape, dim):
    return lax.broadcasted_iota(jnp.int32, shape, dim)


def shape_of(*dims):
    return jax.ShapeDtypeStruct(dims, f32)


def held(*arrays):
    return [pltpu.with_memory_space_constraint(x, pltpu.VMEM) for x in arrays]


def swaps(count, first, ring):
    pairs = []
    for i in range(first, count, 2):
        j = i + 1
        if j == count and not ring:
            break
        pairs += [(i, j % count), (j % count, i)]
    return pairs


def odd_swaps(lat_count, lon_count):
    pairs = []
    for lon in range(lon_count):
        pairs += [(lon * lat_count + i, lon * lat_count + j) for i, j in swaps(lat_count, 1, False)]
        beside = lon + 1 if lon % 2 == 0 else lon - 1
        ends = {0} | ({lat_count - 1} if lat_count % 2 == 0 else set())
        pairs += [(lon * lat_count + end, beside * lat_count + end) for end in sorted(ends)]
    return pairs


def put_rows(blocks, rows, high_side, out):
    levels = blocks[0].shape[0] // rows
    t, q, cx, cy = blocks
    for k, (ref, deep) in enumerate(((t, 0), (t, 1), (q, 0), (q, 1), (cx, 0), (cy, 0))):
        high, low = (ref[pl.ds(r, levels, stride=rows), :] for r in (rows - 1 - deep, deep))
        out[k * levels : (k + 1) * levels, :] = jnp.where(high_side, high, low)


def rows_kernel(rows, tally, perm, *refs):
    count = (len(refs) - 3) // 2
    inputs, (to_a, to_b, sunlit), copies = refs[:count], refs[count : count + 3], refs[count + 3 :]
    even = lax.rem(lax.axis_index("lat"), 2) == 0
    put_rows(inputs[:4], rows, even, to_a)
    put_rows(inputs[:4], rows, jnp.logical_not(even), to_b)
    sunlit[...] = jnp.where(iota(perm.shape, 2) < tally[0, 0], perm[...], -1)
    for ref, copy in zip(inputs, copies):
        copy[...] = ref[...]


def edge_rows(rows, tally, perm, *arrays):
    total, lanes = arrays[0].shape
    sent = HELD((6 * (total // rows), lanes), f32)
    to_a, to_b, sunlit, *copies = pl.pallas_call(
        functools.partial(rows_kernel, rows),
        out_shape=(sent, sent, *(HELD(x.shape, x.dtype) for x in (perm, *arrays))),
        in_specs=[SMEM_SPEC] + [VMEM_SPEC] * (1 + len(arrays)),
        out_specs=(VMEM_SPEC,) * (3 + len(arrays)),
        name="edge_rows",
    )(tally, perm, *arrays)
    return to_a, to_b, (*copies, sunlit)


def halves(x):
    high = x.astype(bf16)
    return high, (x - high.astype(f32)).astype(bf16)


def thirds(value):
    left, parts = np.float32(value), []
    for _ in range(3):
        part = np.float32(left.astype(ml_dtypes.bfloat16))
        parts.append(float(part))
        left = np.float32(left - part)
    return parts


def pick_edges(slots, lanes, blocks):
    zero = jnp.zeros((1, blocks[0].shape[0]), f32)
    edges = [zero] * 16
    for block, at in zip(blocks, slots):
        by_lane = jnp.transpose(block)
        for deep, k in enumerate(at):
            edges[k] = by_lane[lanes - 1 - deep : lanes - deep]
            edges[8 + k] = by_lane[deep : deep + 1]
    return jnp.concatenate(edges, axis=0)


def prepare_kernel(
    pad, t, q, cx, cy, mu, k, albedo, solar, sunlit,
    factor, linear, tables, masks, shares, albedos, scale, ft, fq, fx, fy, own,
):
    levels, gpoints = k.shape
    rows, lanes = mu.shape
    tall = rows + 2 * pad
    blocks = (t, q, cx, cy)
    for ref, out in zip(blocks, (ft, fq, fx, fy)):
        for r in range(rows):
            out[pl.ds(pad + r, levels, stride=tall), :] = ref[pl.ds(r, levels, stride=rows), :]
    own[...] = pick_edges(((0, 1), (2, 3), (4,), (5,)), lanes, [ref[...] for ref in blocks])

    found = jnp.zeros((8, lanes), f32)
    for r in range(rows):
        column = sunlit[0, :, r * lanes : (r + 1) * lanes]
        row_at = jnp.where(column < 0, -1, column // lanes)
        lane_at = lax.rem(column, lanes)
        at_row = jnp.where(row_at == iota((8, lanes), 0), 1.0, 0.0).astype(bf16)
        at_lane = jnp.where(lane_at == iota((lanes, lanes), 0), 1.0, 0.0).astype(bf16)
        found += lax.dot_general(at_row, at_lane, NT_DIMS, preferred_element_type=f32)
    scale[...] = heat_coeff * mu[...] * found[:rows]

    quarter = lanes // 4
    factor[...] = (1.5 + jnp.tanh(q[...])) * (1.0 + 0.25 * jnp.tanh(t[...]))
    ones = jnp.ones((quarter, lanes), bf16)
    for r in range(rows):
        level_factor = factor[pl.ds(r, levels, stride=rows), :]
        per_path = level_factor * (-math.log2(math.e) / mu[r : r + 1, :])
        for start, value in ((0, level_factor), (lanes, per_path)):
            high, low = halves(value)
            linear[start : start + lanes, r * lanes : (r + 1) * lanes] = jnp.concatenate(
                [high, high, low, ones], axis=0
            )
    square = iota((gpoints, gpoints), 0) == iota((gpoints, gpoints), 1)

    def upright(row):
        return jnp.sum(jnp.where(square, row, 0.0), axis=1, keepdims=True)

    w = upright(albedo[...])
    filled = jnp.concatenate([k[...], jnp.zeros((levels, lanes - gpoints), f32)], axis=1)
    coeff = jnp.transpose(filled)[:gpoints]
    slot = iota((1, quarter), 1)

    def table(value, constants):
        high = value.astype(bf16).astype(f32)
        tail = jnp.zeros((1, quarter), f32)
        for i, c in enumerate(constants):
            tail = jnp.where(slot == i, c, tail)
        tail = jnp.broadcast_to(tail, (gpoints, quarter))
        return jnp.concatenate([high, value - high, high, tail], axis=1).astype(bf16)

    tables[0] = table(coeff, thirds(1.0 / 3.0))
    tables[1] = table(1.5 * (1.0 - w) * coeff, (0.75,))
    shares[...] = (1.0 - w) * upright(solar[...]) * coeff
    albedos[...] = jnp.broadcast_to(1.5 * w, (gpoints, lanes))
    lane = iota((16, lanes), 1)
    level, constant = lax.rem(lane, quarter), lane >= 3 * quarter
    for l in range(levels):
        masks[0, l] = jnp.where(constant | (level == l) | (level == l + 1), 1.0, 0.0).astype(bf16)
        masks[1, l] = jnp.where(constant | (level == l), 1.0, 0.0).astype(bf16)
        masks[2, l] = jnp.where(
            constant, 0.0, jnp.where(level < l, 1.0, jnp.where(level == l, 0.5, 0.0))
        ).astype(bf16)


def prepare(t, q, cx, cy, mu, k, albedo, solar, sunlit, pad):
    levels, gpoints = k.shape
    rows, lanes = mu.shape
    tall = levels * (rows + 2 * pad)
    return pl.pallas_call(
        functools.partial(prepare_kernel, pad),
        out_shape=(
            HELD(t.shape, f32),
            HELD((2 * lanes, rows * lanes), bf16),
            HELD((2, gpoints, lanes), bf16),
            HELD((3, levels, 16, lanes), bf16),
            HELD((gpoints, levels), f32),
            HELD((gpoints, lanes), f32),
            HELD((rows, lanes), f32),
            *[HELD((tall, lanes), f32)] * 4,
            HELD((16, levels * rows), f32),
        ),
        in_specs=[VMEM_SPEC] * 9,
        out_specs=(VMEM_SPEC,) * 12,
        cost_estimate=pl.CostEstimate(flops=1 << 22, bytes_accessed=1 << 21, transcendentals=1 << 17),
        name="prepare",
    )(*held(t, q, cx, cy, mu, k, albedo, solar, sunlit))


def by_side(even, first, last, from_a, from_b, k, levels, low, high):
    a, b = from_a[k * levels : (k + 1) * levels, :], from_b[k * levels : (k + 1) * levels, :]
    south, north = jnp.where(even, b, a), jnp.where(even, a, b)
    return jnp.where(first, low, south), jnp.where(last, high, north)


def lat_place():
    lat = lax.axis_index("lat")
    return lax.rem(lat, 2) == 0, lat == 0, lat == lax.axis_size("lat") - 1


def columns_kernel(pad, ft, fq, own, from_a, from_b, _, edges, to_a, to_b, ring):
    levels = from_a.shape[0] // 6
    total, lanes = ring.shape[1:]
    rows = total // levels
    tall = rows + 2 * pad
    ring[...] = jnp.zeros_like(ring)
    for i, ref in enumerate((ft, fq)):
        low, high = (ref[pl.ds(pad + r, levels, stride=tall), :] for r in (0, rows - 1))
        south, north = by_side(*lat_place(), from_a, from_b, 2 * i, levels, low, high)
        ring[i, pl.ds(0, levels, stride=rows), :] = south
        ring[i, pl.ds(rows - 1, levels, stride=rows), :] = north
    both = own[...] + pick_edges(((6,), (7,)), lanes, [ring[0], ring[1]])
    edges[...] = both
    even_lon = lax.rem(lax.axis_index("lon"), 2) == 0
    east, west = both[:8], both[8:]
    to_a[...] = jnp.where(even_lon, east, west)
    to_b[...] = jnp.where(even_lon, west, east)


def edge_columns(ft, fq, own, from_a, from_b, after, rows, pad):
    lanes = ft.shape[1]
    total = own.shape[1]
    return pl.pallas_call(
        functools.partial(columns_kernel, pad),
        out_shape=(HELD((16, total), f32), HELD((8, total), f32), HELD((8, total), f32)),
        in_specs=[VMEM_SPEC] * 6,
        out_specs=(VMEM_SPEC,) * 3,
        scratch_shapes=[pltpu.VMEM((2, total, lanes), f32)],
        name="edge_columns",
    )(*held(ft, fq, own, from_a, from_b, after))


def weights(cx, cy):
    hx, hy = 0.5 * cx, 0.5 * cy
    sx, sy = hx * cx, hy * cy
    return 1.0 - 2.0 * (sx + sy), sx - hx, sx + hx, sy - hy, sy + hy


def blend(w, here, east, west, north, south):
    return w[0] * here + w[1] * east + w[2] * west + w[3] * north + w[4] * south


def advect_kernel(
    rows, pad, ft, fq, fx, fy, edges, lat_a, lat_b, lon_a, lon_b, t_out, q_out, gt, gq, gx, gy, st, sq
):
    lanes = ft.shape[1]
    high = rows + 2 * pad
    levels = ft.shape[0] // high
    total = levels * rows
    place = lat_place()
    _, first, last = place
    grids = (gt, gq, gx, gy)
    for ref, grid, at in zip((ft, fq, fx, fy), grids, ((0, 1), (2, 3), (4,), (5,))):
        grid[...] = ref[...]
        low, top = (ref[pl.ds(pad + r, levels, stride=high), :] for r in (0, rows - 1))
        for deep in range(pad):
            k = at[min(deep, len(at) - 1)]
            south, north = by_side(*place, lat_a, lat_b, k, levels, low, top)
            grid[pl.ds(pad - 1 - deep, levels, stride=high), :] = south
            grid[pl.ds(pad + rows + deep, levels, stride=high), :] = north
    even_lon = lax.rem(lax.axis_index("lon"), 2) == 0
    a, b = lon_a[...], lon_b[...]
    east, west = jnp.where(even_lon, a, b), jnp.where(even_lon, b, a)
    mine = edges[...]

    def strip(x, k):
        return x[k : k + 1, :]

    row_of = lax.rem(iota((1, total), 1), rows)

    def up(x, k):
        return jnp.where(row_of == rows - 1, strip(x, 6 + k // 2), pltpu.roll(strip(x, k), total - 1, 1))

    def down(x, k):
        return jnp.where(row_of == 0, strip(x, 6 + k // 2), pltpu.roll(strip(x, k), 1, 1))

    ww = weights(strip(west, 4), strip(west, 5))
    we = weights(strip(east, 4), strip(east, 5))
    firsts = []
    for k in (0, 2):
        firsts.append(blend(ww, strip(west, k), strip(mine, 8 + k), strip(west, k + 1), up(west, k), down(west, k)))
        firsts.append(blend(we, strip(east, k), strip(east, k + 1), strip(mine, k), up(east, k), down(east, k)))
    columns = [strip(x, k) for k in (0, 2, 6, 7) for x in (east, west)]
    columns += [firsts[i] for i in (1, 0, 3, 2)]
    stack = jnp.concatenate(columns + [jnp.zeros((lanes - len(columns), total), f32)], axis=0)
    by_lane = jnp.transpose(stack)
    spread = (st, sq)
    cut = lambda x: x.reshape(levels, high, lanes)
    flat = lambda i: pltpu.roll(by_lane, lanes - 1 - 2 * i, 1)
    w = weights(cut(gx[...]), cut(gy[...]))
    full = (levels, high, lanes)
    lane, at = iota(full, 2), iota(full, 1)
    for k, (ref, out, rim_ref) in enumerate(((gt, t_out, st), (gq, q_out, sq))):
        f = cut(ref[...])
        for step in range(2):
            rim_ref[step, 0] = flat((0, 4)[step] + k)
            if step == 0:
                rim_ref[step, 1] = flat(2 + k)
            tall_rim = ref
            for r in range(rows):
                tall_rim[pl.ds(pad + r, levels, stride=high), :] = rim_ref[step, 0, pl.ds(r, levels, stride=rows), :]
            if step == 0:
                tall_rim[pl.ds(pad - 1, levels, stride=high), :] = rim_ref[step, 1, pl.ds(0, levels, stride=rows), :]
                tall_rim[pl.ds(pad + rows, levels, stride=high), :] = rim_ref[
                    step, 1, pl.ds(rows - 1, levels, stride=rows), :
                ]
            rim = cut(tall_rim[...])
            e = jnp.where(lane == lanes - 1, rim, pltpu.roll(f, lanes - 1, 2))
            wst = jnp.where(lane == 0, rim, pltpu.roll(f, 1, 2))
            n = jnp.where(last & (at == pad + rows - 1), f, pltpu.roll(f, high - 1, 1))
            s = jnp.where(first & (at == pad), f, pltpu.roll(f, 1, 1))
            f = blend(w, f, e, wst, n, s)
        ref[...] = f.reshape(levels * high, lanes)
        for r in range(rows):
            out[pl.ds(r, levels, stride=rows), :] = ref[pl.ds(pad + r, levels, stride=high), :]


def advect(ft, fq, fx, fy, edges, lat_a, lat_b, lon_a, lon_b, rows, pad):
    tall, lanes = ft.shape
    total = edges.shape[1]
    grid = pltpu.VMEM((tall, lanes), f32)
    return pl.pallas_call(
        functools.partial(advect_kernel, rows, pad),
        out_shape=(shape_of(total, lanes), shape_of(total, lanes)),
        in_specs=[VMEM_SPEC] * 9,
        out_specs=(VMEM_SPEC,) * 2,
        scratch_shapes=[grid] * 4 + [pltpu.VMEM((2, 2, total, lanes), f32)] * 2,
        name="advect",
    )(*held(ft, fq, fx, fy, edges, lat_a, lat_b, lon_a, lon_b))

SLOTS, AHEAD = 16, 8
EARLY = 5


def row_sums(tiles):
    row = iota(tiles[0].shape, 0)
    for far in (4, 2, 1):
        low = (row & far) == 0
        merged = []
        for a, b in zip(tiles[:far], tiles[far:]):
            other = jnp.where(low, b, a)
            back = pltpu.roll(other, far, 0)
            if far != 4:
                back = jnp.where(low, pltpu.roll(other, 8 - far, 0), back)
            merged.append(jnp.where(low, a, b) + back)
        tiles = merged
    return tiles[0]


def heating_kernel(
    begin, end, linear, tables, masks, shares, albedos, *refs
):
    gpoints, levels = shares.shape
    lanes = albedos.shape[1]
    rows = linear.shape[1] // lanes
    if begin == 0:
        total, trans, pull, beam = refs
    else:
        so_far, factor, scale, _, out, trans, pull, beam, total = refs
    wide = 2 * lanes
    engines = rows // 2
    units = [(a, b) for a in range(2) for b in range(rows)]
    each = range(len(units))

    def main(*sums):
        def at(m, l):
            return sums[m * SLOTS + l % SLOTS]

        blank = jnp.zeros((16, lanes), bf16)

        def issue(i, l):
            start = pl.multiple_of(i * 16, 16)
            plain, absorbing = (tables[j, pl.ds(start, 16), :] for j in range(2))
            stack = [
                jnp.concatenate([plain * masks[0, l], blank], axis=1),
                jnp.concatenate([absorbing * masks[1, l], blank], axis=1),
                jnp.concatenate([blank, plain * masks[2, l]], axis=1),
            ]
            stack = jnp.concatenate(stack, axis=0)
            for m in range(engines):
                pltpu.matmul_acc_lhs(at(m, l), stack)

        def group(i, more=True, opening=False):
            start = pl.multiple_of(i * 16, 16)
            starts = [pl.multiple_of(start + 8 * a, 8) for a in range(2)]
            w15 = [albedos[pl.ds(s, 8), :] for s in starts]
            share = [shares[pl.ds(s, 8), :] for s in starts]
            y = current = step = None
            for l in range(levels):
                if l + AHEAD < levels:
                    issue(i, l + AHEAD)
                popped = [pltpu.matmul_pop(at(m, l)) for m in range(engines)]

                def part(kind, a, b):
                    s = kind * 16 + a * 8
                    return popped[b // 2][s : s + 8, (b % 2) * lanes : (b % 2 + 1) * lanes]

                resist, shunt, path = ([part(i, a, b) for a, b in units] for i in range(3))
                direct = [jnp.exp2(p) for p in path]
                source = [w15[units[u][0]] * direct[u] for u in each]
                for u in each:
                    beam[u, l] = direct[u]
                if l == 0:
                    y, current = shunt, source
                else:
                    y = [shunt[u] + y[u] * step[u] for u in each]
                    current = [source[u] + current[u] * step[u] for u in each]
                if l < levels - 1:
                    step = [1.0 / (1.0 + resist[u] * y[u]) for u in each]
                    for u in each:
                        trans[u, l] = step[u]
                        pull[u, l] = resist[u] * current[u]
            diffuse = [current[u] / y[u] for u in each]
            for l in range(levels - 1, -1, -1):
                if more and levels - 1 - l < AHEAD:
                    issue(i + 1, levels - 1 - l)
                if l < levels - 1:
                    diffuse = [trans[u, l] * (pull[u, l] + diffuse[u]) for u in each]
                spread = [jnp.broadcast_to(share[a][:, l : l + 1], (8, lanes)) for a in range(2)]
                for b in range(rows):
                    pair = [
                        (diffuse[a * rows + b] + beam[a * rows + b, l]) * spread[a]
                        for a in range(2)
                    ]
                    both = pair[0] + pair[1]
                    if not opening:
                        both = total[l, b] + both
                    elif begin > 0:
                        both = so_far[l, b] + both
                    total[l, b] = both

        nothing = jnp.zeros((16, wide), bf16)
        for m in range(engines):
            last = sums[engines * SLOTS + m]
            pltpu.matmul_push_rhs(linear[:, m * wide : (m + 1) * wide], 0, m)
            pltpu.matmul_acc_lhs(last, nothing, load_staged_rhs=0)
            pltpu.matmul_pop(last)
        for l in range(AHEAD):
            issue(begin, l)
        group(begin, more=end - begin > 1, opening=True)
        if end - begin > 2:
            pl.loop(begin + 1, end - 1)(group)
        if end - begin > 1:
            group(end - 1, more=False)

    pl.run_scoped(
        main,
        *[pltpu.ACC(m)((48, wide), f32) for m in range(engines) for _ in range(SLOTS)],
        *[pltpu.ACC(m)((16, wide), f32) for m in range(engines)],
    )
    if begin == 0:
        return
    block = 8 // rows
    column_scale = jnp.concatenate([scale[...]] * block, axis=0)
    for l in range(0, levels, block):
        here = pl.ds(l * rows, 8)
        sums = row_sums([total[l + i, r] for i in range(block) for r in range(rows)])
        out[here, :] = sums * column_scale * factor[here, :]


def heating(linear, tables, masks, shares, albedos, begin, end, more=()):
    gpoints, levels = shares.shape
    lanes = albedos.shape[1]
    rows = linear.shape[1] // lanes
    stage = pltpu.VMEM((2 * rows, levels, 8, lanes), f32)
    sums = (levels, rows, 8, lanes)
    cells = (end - begin) * 16 * levels * rows * lanes
    return pl.pallas_call(
        functools.partial(heating_kernel, begin, end),
        out_shape=shape_of(levels * rows, lanes) if more else HELD(sums, f32),
        in_specs=[VMEM_SPEC] * (5 + len(more)),
        out_specs=VMEM_SPEC,
        scratch_shapes=[stage, stage, stage] + [pltpu.VMEM(sums, f32)] * bool(more),
        cost_estimate=pl.CostEstimate(flops=640 * cells, bytes_accessed=1 << 20, transcendentals=2 * cells),
        name="heating",
    )(*held(linear, tables, masks, shares, albedos, *more))


def local(
    thermal_deviation,
    moisture_deviation,
    eastward_stability,
    northward_stability,
    sun_height_ratio,
    extinction_coeff,
    reflectivity_ratio,
    insolation_source,
    daylight_tally,
    daylight_permutation,
):
    levels, rows, lanes = thermal_deviation.shape
    pad = 2
    lat_count, lon_count = lax.axis_size("lat"), lax.axis_size("lon")
    flat = lambda x: x.reshape(levels * rows, lanes)
    t, q, cx, cy = (
        flat(x)
        for x in (thermal_deviation, moisture_deviation, eastward_stability, northward_stability)
    )
    to_a, to_b, copies = edge_rows(
        rows,
        daylight_tally,
        daylight_permutation,
        t,
        q,
        cx,
        cy,
        sun_height_ratio,
        jnp.transpose(extinction_coeff),
        reflectivity_ratio.reshape(1, -1),
        insolation_source.reshape(1, -1),
    )
    lat_a = lax.ppermute(to_a, "lat", swaps(lat_count, 0, False))
    lat_b = lax.ppermute(to_b, ("lon", "lat"), odd_swaps(lat_count, lon_count))
    factor, *tables, scale, ft, fq, fx, fy, own = prepare(*copies, pad)
    groups = extinction_coeff.shape[0] // 16
    early = min(EARLY, groups - 1)
    sums = heating(*tables, 0, early)
    edges, to_a, to_b = edge_columns(ft, fq, own, lat_a, lat_b, sums, rows, pad)
    lon_b = lax.ppermute(to_b, "lon", swaps(lon_count, 1, True))
    lon_a = lax.ppermute(to_a, "lon", swaps(lon_count, 0, True))
    warming = heating(*tables, early, groups, (sums, factor, scale, edges))
    t_next, q_next = advect(ft, fq, fx, fy, edges, lat_a, lat_b, lon_a, lon_b, rows, pad)
    whole = lambda x: x.reshape(levels, rows, lanes)
    return whole(t_next), whole(q_next), whole(warming)


def solution(mesh):
    volume, surface = P(None, "lat", "lon"), P("lat", "lon")
    placed = (volume,) * 4 + (surface, P(), P(), P(), surface, P("lat", "lon", None))
    step = jax.shard_map(
        local, mesh=mesh, in_specs=placed, out_specs=(volume,) * 3, check_vma=False
    )
    return step
```
